128 devices in a mesh: tok: 64 (over x, y, z), head: 2 (over core).
Axes of the slice: x: 4, y: 4, z: 4, core: 2. Of those that a mesh axis runs over, the one named last changes fastest.
Arguments:
- queries: bfloat16 [2, 49152, 1536], P(None, 'tok', 'head'), may hold values from -16 to 16
- key_rows: bfloat16 [2, 49152, 1536], P(None, 'tok', 'head'), may hold values from -8 to 8
- value_rows: bfloat16 [2, 49152, 1536], P(None, 'tok', 'head'), may hold values from -6 to 6
- step_rates: float32 [4, 2, 49152], P('head', None, 'tok'), may hold values from 0.01 to 1
- gate_init: float32 [4, 384, 384], P('head'), may hold values from -0.3125 to 0.3125
- up_init: float32 [4, 384, 384], P('head'), may hold values from -0.3125 to 0.3125
- down_init: float32 [4, 384, 384], P('head'), may hold values from -0.3125 to 0.3125
- out_weight: bfloat16 [1536, 1536], P('head'), may hold values from -0.15625 to 0.15625
Outputs:
- mixed_out: bfloat16 [2, 49152, 1536], P(None, 'tok', 'head')
The draws below stay inside these ranges and needn't reach their ends.
All inputs are finite; a program needn't handle non-finite values.
Results may differ from the reference program's by a relative error of at most 0.009.
Values may be sent and summed in bfloat16 or wider, within the bound.
No kernel may reach another device: no remote copies, remote signals or barrier semaphores. Data moves between devices by JAX's collectives and lax.ppermute only.
A program may use at most 128 MiB of HBM per device.

```python
import math
import jax
import jax.numpy as jnp
from jax import lax

D = 1536
HEADS = 4
DH = 384
FH = 384
WINDOW = 384
BLOCKS = 2
BLOCK = 49152


def draw_pair(base_key):
    shape = (BLOCKS, BLOCK, HEADS * DH)
    keyed = jax.random.fold_in(base_key, 7177)
    first_key, second_key = jax.random.split(keyed, 2)
    query_draw = jnp.clip(jax.random.normal(first_key, shape, jnp.float32), -8.0, 8.0)
    key_draw = jnp.clip(jax.random.normal(second_key, shape, jnp.float32), -8.0, 8.0)
    return (query_draw, key_draw)


def draw_queries(key, part):
    return draw_pair(key)[0].astype(jnp.bfloat16)


def draw_key_rows(key, part):
    return draw_pair(key)[1].astype(jnp.bfloat16)


def draw_step_rates(key, part):
    shape = (HEADS, BLOCKS, BLOCK)
    keyed = jax.random.fold_in(key, 9311)
    unit = jax.random.uniform(keyed, shape, jnp.float32)
    position = jnp.arange(BLOCK).astype(jnp.float32) / (BLOCK - 1)
    ramp = jnp.exp(jnp.log(0.15) * (1.0 - position))
    factor = jnp.exp(jnp.log(0.1) * (1.0 - unit))
    return (factor * ramp[None, None, :]).astype(jnp.float32)


def block_scale(own_key, shape, pieces, low, top_value):
    gain = 1.0
    for dim, blocks in pieces:
        heights = jax.random.uniform(jax.random.fold_in(jax.random.fold_in(own_key, 6), dim), (blocks,), jnp.float32, low / len(pieces), top_value / len(pieces))
        gain = gain * jnp.repeat(jnp.exp(heights), shape[dim] // blocks).reshape((-1,) + (1,) * (len(shape) - 1 - dim))
    return gain


def centred(rng, dims, deviation, most, cuts=(), kind=jnp.bfloat16):
    drawn = jax.random.normal(rng, dims, jnp.float32) * deviation
    if len(cuts) > 0:
        drawn = block_scale(rng, dims, cuts, -0.22, 0.18) * drawn
    return jnp.clip(drawn, min=-most, max=most).astype(kind)


def setup_inputs(seed: int = 0) -> dict:
    key_list = jax.random.split(jax.random.key(seed), 9)
    queries = draw_queries(jax.random.fold_in(key_list[8], 71), 0)
    key_rows = draw_key_rows(jax.random.fold_in(key_list[8], 71), 0)
    value_rows = centred(key_list[2], (BLOCKS, BLOCK, HEADS * DH), 1.0, 6.0, ((1, 64), (2, 2)))
    step_rates = draw_step_rates(jax.random.fold_in(key_list[8], 71), 0)
    gate_init = centred(key_list[4], (HEADS, FH, DH), DH ** -0.5, 0.3125, ((0, 2),), jnp.float32)
    up_init = centred(key_list[5], (HEADS, FH, DH), DH ** -0.5, 0.3125, ((0, 2),), jnp.float32)
    down_init = centred(key_list[6], (HEADS, DH, FH), FH ** -0.5, 0.3125, ((0, 2),), jnp.float32)
    out_weight = centred(key_list[7], (HEADS * DH, D), (HEADS * DH) ** -0.5, 0.15625, ((0, 2),))
    return {"queries": queries, "key_rows": key_rows, "value_rows": value_rows, "step_rates": step_rates, "gate_init": gate_init, "up_init": up_init, "down_init": down_init, "out_weight": out_weight}


EPSILON = 1e-06

def silu_slope(values_in):
    sigmoid_at = jax.nn.sigmoid(values_in)
    return sigmoid_at * (1.0 + values_in * (1.0 - sigmoid_at))

def row_scale(matrix):
    return jnp.sqrt(lax.optimization_barrier(jnp.mean(matrix * matrix, axis=-1, keepdims=True)) + EPSILON)

def renormed(old_weight, gradient, rate_sum):
    updated = old_weight - gradient / rate_sum
    return updated * (row_scale(old_weight) / row_scale(updated))

def window_attention(queries, key_rows, value_rows):
    length = queries.shape[0] * queries.shape[1]
    flat_queries = queries.reshape(length, HEADS, DH)
    zero_rows = jnp.zeros((WINDOW, HEADS, DH), jnp.bfloat16)
    flat_keys = jnp.concatenate([zero_rows, key_rows.reshape(length, HEADS, DH)], axis=0)
    flat_values = jnp.concatenate([zero_rows, value_rows.reshape(length, HEADS, DH)], axis=0)
    score_scale = 1.0 / math.sqrt(DH)

    def one_block(block_index):
        first_row = (block_index * WINDOW).astype(jnp.int32)
        query_block = lax.dynamic_slice_in_dim(flat_queries, first_row, WINDOW, 0).astype(jnp.float32)
        key_block = lax.dynamic_slice_in_dim(flat_keys, first_row, 2 * WINDOW, 0).astype(jnp.float32)
        value_block = lax.dynamic_slice_in_dim(flat_values, first_row, 2 * WINDOW, 0).astype(jnp.float32)
        scores = jnp.einsum('qhd,khd->hqk', query_block, key_block) * score_scale
        offset = jnp.arange(2 * WINDOW)[None, :] - WINDOW - jnp.arange(WINDOW)[:, None]
        global_key = first_row + jnp.arange(2 * WINDOW) - WINDOW
        allowed = (offset <= 0) & (offset > -WINDOW) & (global_key >= 0)[None, :]
        scores = jnp.where(allowed[None], scores, -jnp.inf)
        row_max = lax.optimization_barrier(jnp.max(scores, axis=-1, keepdims=True))
        expos = jnp.exp(scores - row_max)
        weights_bf = (expos / lax.optimization_barrier(jnp.sum(expos, axis=-1, keepdims=True))).astype(jnp.bfloat16)
        return jnp.einsum('hqk,khd->qhd', weights_bf.astype(jnp.float32), value_block)
    results = lax.map(one_block, jnp.arange(length // WINDOW, dtype=jnp.int32))
    return results.reshape(queries.shape[0], queries.shape[1], HEADS, DH)

def reference(queries, key_rows, value_rows, step_rates, gate_init, up_init, down_init, out_weight):
    attention = window_attention(queries, key_rows, value_rows)
    gate_now, up_now, down_now = (gate_init, up_init, down_init)
    outputs = []
    for block_at in range(BLOCKS):
        head_list = []
        gate_list, up_list, down_list = ([], [], [])
        for head_at in range(HEADS):
            lower = head_at * DH
            key_now = key_rows[block_at][:, lower:lower + DH]
            value_now = value_rows[block_at][:, lower:lower + DH]
            query_now = queries[block_at][:, lower:lower + DH]
            rate_now = step_rates[head_at, block_at]
            cast_gate = gate_now[head_at].astype(jnp.bfloat16)
            cast_up = up_now[head_at].astype(jnp.bfloat16)
            cast_down = down_now[head_at].astype(jnp.bfloat16)
            errors = (rate_now[:, None] * value_now.astype(jnp.float32)).astype(jnp.bfloat16)
            pre_gate = jnp.dot(key_now, cast_gate.T, preferred_element_type=jnp.float32)
            pre_up = jnp.dot(key_now, cast_up.T, preferred_element_type=jnp.float32)
            active = jax.nn.silu(pre_gate)
            hidden = (active * pre_up).astype(jnp.bfloat16)
            backed = jnp.dot(errors, cast_down, preferred_element_type=jnp.float32)
            back_up = (-backed * active).astype(jnp.bfloat16)
            back_gate = (-backed * pre_up * silu_slope(pre_gate)).astype(jnp.bfloat16)
            grad_gate = jnp.dot(back_gate.T, key_now, preferred_element_type=jnp.float32)
            grad_up = jnp.dot(back_up.T, key_now, preferred_element_type=jnp.float32)
            grad_down = -jnp.dot(errors.T, hidden, preferred_element_type=jnp.float32)
            rate_total = jnp.sum(rate_now)
            new_gate = renormed(gate_now[head_at], grad_gate, rate_total)
            new_up = renormed(up_now[head_at], grad_up, rate_total)
            new_down = renormed(down_now[head_at], grad_down, rate_total)
            query_gate = jnp.dot(query_now, new_gate.astype(jnp.bfloat16).T, preferred_element_type=jnp.float32)
            query_up = jnp.dot(query_now, new_up.astype(jnp.bfloat16).T, preferred_element_type=jnp.float32)
            query_hidden = (jax.nn.silu(query_gate) * query_up).astype(jnp.bfloat16)
            fast_out = jnp.dot(query_hidden, new_down.astype(jnp.bfloat16).T, preferred_element_type=jnp.float32)
            fast_out = fast_out / row_scale(fast_out)
            head_list.append((fast_out + attention[block_at, :, head_at, :]).astype(jnp.bfloat16))
            gate_list.append(new_gate)
            up_list.append(new_up)
            down_list.append(new_down)
        gate_now = jnp.stack(gate_list)
        up_now = jnp.stack(up_list)
        down_now = jnp.stack(down_list)
        outputs.append(jnp.concatenate(head_list, axis=1))
    joined = jnp.stack(outputs).reshape(BLOCKS * BLOCK, HEADS * DH)
    mixed_out = jnp.dot(joined, out_weight, preferred_element_type=jnp.float32).astype(jnp.bfloat16)
    return mixed_out.reshape(BLOCKS, BLOCK, D)
```

```python
import functools
import math

import jax
import jax.numpy as jnp
from jax import lax
from jax.experimental import pallas as pl
from jax.experimental.pallas import tpu as pltpu
from jax.sharding import PartitionSpec as P

DH = 384
WINDOW = 384
EPSILON = 1e-06
BF16 = jnp.bfloat16
F32 = jnp.float32
TOKENS_AT_ONCE = 256
QUERY_TILE = 128

NT = (((1,), (1,)), ((), ()))
NN = (((1,), (0,)), ((), ()))


def dot(a, b, dims):
    return lax.dot_general(a, b, dims, preferred_element_type=F32)


def cost(flops, bytes_accessed, transcendentals=0):
    return pl.CostEstimate(
        flops=int(flops), bytes_accessed=int(bytes_accessed), transcendentals=int(transcendentals)
    )


def load_packed(packed_ref, flat, rows):
    for at in range(packed_ref.shape[0]):
        flat[at * rows : (at + 1) * rows, :] = packed_ref[at, :rows, :].astype(F32)


def gradient_kernel(first, block_at, rows, *refs):
    if first:
        key_ref, value_ref, rate_ref, gate_ref, up_ref, down_ref, out_ref, flat, sums = refs
        gate, up = gate_ref[...].astype(BF16), up_ref[...].astype(BF16)
        down_t = jnp.transpose(down_ref[...]).astype(BF16)
    else:
        key_ref, value_ref, rate_ref, packed_ref, out_ref, flat, sums = refs
        load_packed(packed_ref, flat, rows)
        gate, up = flat[:DH, :].astype(BF16), flat[DH : 2 * DH, :].astype(BF16)
        down_t = jnp.transpose(flat[2 * DH :, :]).astype(BF16)
    tokens = key_ref.shape[0]
    rates = rate_ref[block_at : block_at + 1, :]
    for at in range(tokens // TOKENS_AT_ONCE):
        piece = slice(at * TOKENS_AT_ONCE, (at + 1) * TOKENS_AT_ONCE)
        key, value = key_ref[piece, :], value_ref[piece, :]
        rate = rates[:, piece]
        pre_gate = dot(gate, key, NT)
        pre_up = dot(up, key, NT)
        backed = dot(down_t, value, NT) * rate
        sigmoid = jax.nn.sigmoid(pre_gate)
        active = pre_gate * sigmoid
        hidden = (active * pre_up * rate).astype(BF16)
        to_up = (backed * active).astype(BF16)
        slope = sigmoid * (1.0 + pre_gate * (1.0 - sigmoid))
        to_gate = (backed * pre_up * slope).astype(BF16)
        for which, (left, right) in enumerate(((to_gate, key), (to_up, key), (hidden, value))):
            term = dot(left, right, NN)
            if at == 0:
                sums[which] = term
            else:
                sums[which] += term
    flat[:DH, :] = sums[0]
    flat[DH : 2 * DH, :] = sums[1]
    flat[2 * DH :, :] = jnp.transpose(sums[2])
    total = jnp.sum(rates, axis=1, keepdims=True)
    high = total.astype(BF16)
    low = (total - high.astype(F32)).astype(BF16)
    extra = out_ref.shape[1] - rows
    place = lax.broadcasted_iota(jnp.int32, (extra, DH), 0)
    tail = jnp.where(place == 0, high.astype(F32), jnp.where(place == 1, low.astype(F32), 0.0))
    for at in range(out_ref.shape[0]):
        piece = jnp.concatenate([flat[at * rows : (at + 1) * rows, :], tail], axis=0)
        out_ref[at] = piece.astype(BF16)


def gradients(block_at, key_rows, value_rows, step_rates, weights, shards, rows, padded):
    _, tokens, width = key_rows.shape
    heads = width // DH
    first = len(weights) == 3
    matrix = pl.BlockSpec((None, DH, DH), lambda h: (h, 0, 0))
    per_head = shards // heads
    packed = pl.BlockSpec((per_head, padded, DH), lambda h: (h, 0, 0))
    rowed = pl.BlockSpec((None, tokens, DH), lambda h: (block_at, 0, h))
    return pl.pallas_call(
        functools.partial(gradient_kernel, first, block_at, rows),
        grid=(heads,),
        in_specs=[rowed, rowed, pl.BlockSpec((None, step_rates.shape[1], tokens), lambda h: (h, 0, 0))]
        + ([matrix] * 3 if first else [packed]),
        out_specs=packed,
        out_shape=jax.ShapeDtypeStruct((shards, padded, DH), BF16),
        scratch_shapes=[pltpu.VMEM((3 * DH, DH), F32), pltpu.VMEM((3, DH, DH), F32)],
        cost_estimate=cost(heads * 12 * tokens * DH * DH, 8e6, heads * tokens * DH * 2),
        name="gradients",
    )(key_rows, value_rows, step_rates, *weights)


def row_scale(matrix):
    return jnp.sqrt(jnp.mean(matrix * matrix, axis=-1, keepdims=True) + EPSILON)


def update_kernel(rows, parts_ref, old_ref, new_ref, copies_ref):
    total = parts_ref[0].astype(F32)
    for at in range(1, parts_ref.shape[0]):
        total += parts_ref[at].astype(F32)
    rate = total[rows : rows + 1, :] + total[rows + 1 : rows + 2, :]
    old = old_ref[...]
    updated = old + total / rate
    new = updated * (row_scale(old) / row_scale(updated))
    new_ref[...] = new
    rounded = new.astype(BF16)
    for at in range(copies_ref.shape[0]):
        copies_ref[at] = rounded


def update(parts, old, rows):
    shards, padded, _ = parts.shape
    return pl.pallas_call(
        functools.partial(update_kernel, rows),
        out_shape=(
            jax.ShapeDtypeStruct((padded, DH), F32),
            jax.ShapeDtypeStruct((shards, padded, DH), BF16),
        ),
        in_specs=[pl.BlockSpec(memory_space=pltpu.VMEM)] * 2,
        out_specs=(pl.BlockSpec(memory_space=pltpu.VMEM),) * 2,
        cost_estimate=cost(2 * shards * padded * DH, 4e6),
        name="update",
    )(parts, old)


def attend(query_ref, keys, values, out_ref, barred):
    scale = 1.0 / math.sqrt(DH)
    span = WINDOW + QUERY_TILE
    row = lax.broadcasted_iota(jnp.int32, (QUERY_TILE, span), 0)
    column = lax.broadcasted_iota(jnp.int32, (QUERY_TILE, span), 1)
    window = (column > row) & (column <= row + WINDOW)
    for at in range(query_ref.shape[0] // QUERY_TILE):
        low = at * QUERY_TILE
        scores = dot(query_ref[low : low + QUERY_TILE, :], keys[low : low + span, :], NT) * scale
        allowed = window if barred is None else window & (column + low >= barred)
        scores = jnp.where(allowed, scores, -jnp.inf)
        expos = jnp.exp(scores - jnp.max(scores, axis=1, keepdims=True))
        weights = (expos * (1.0 / jnp.sum(expos, axis=1, keepdims=True))).astype(BF16)
        out_ref[low : low + QUERY_TILE, :] = dot(weights, values[low : low + span, :], NN)


def local_kernel(query_ref, key_ref, value_ref, out_ref):
    attend(query_ref, key_ref, value_ref, out_ref, None)


def attention_cost(blocks, heads):
    pairs = blocks * heads * WINDOW * (WINDOW + QUERY_TILE)
    return cost(4 * pairs * DH, 10e6, pairs)


def local_attention(queries, key_rows, value_rows):
    blocks, tokens, width = queries.shape
    heads = width // DH
    last = tokens // WINDOW - 1
    return pl.pallas_call(
        local_kernel,
        grid=(blocks, heads),
        in_specs=[
            pl.BlockSpec((None, WINDOW, DH), lambda b, h: (b, last, h)),
            pl.BlockSpec((None, tokens, DH), lambda b, h: (b, 0, h)),
            pl.BlockSpec((None, tokens, DH), lambda b, h: (b, 0, h)),
        ],
        out_specs=pl.BlockSpec((None, WINDOW, DH), lambda b, h: (b, 0, h)),
        out_shape=jax.ShapeDtypeStruct((blocks, WINDOW, width), F32),
        cost_estimate=attention_cost(blocks, heads),
        name="local_attention",
    )(queries, key_rows, value_rows)


def near_kernel(place_ref, query_ref, near_key, near_value, key_ref, value_ref, out_ref, keys, values):
    keys[:WINDOW, :] = near_key[...]
    keys[WINDOW:, :] = key_ref[...]
    values[:WINDOW, :] = near_value[...]
    values[WINDOW:, :] = value_ref[...]
    absent = (place_ref[0] == 0) & (pl.program_id(0) == 0)
    attend(query_ref, keys, values, out_ref, jnp.where(absent, WINDOW, 0))


def near_attention(place, queries, near_keys, near_values, key_rows, value_rows):
    blocks, _, width = queries.shape
    heads = width // DH
    own = pl.BlockSpec((None, WINDOW, DH), lambda b, h, place: (b, 0, h))
    near = pl.BlockSpec(
        (None, WINDOW, DH),
        lambda b, h, place: (jnp.where(place[0] == 0, jnp.maximum(b - 1, 0), b), 0, h),
    )
    return pl.pallas_call(
        near_kernel,
        grid_spec=pltpu.PrefetchScalarGridSpec(
            num_scalar_prefetch=1,
            grid=(blocks, heads),
            in_specs=[own, near, near, own, own],
            out_specs=own,
            scratch_shapes=[pltpu.VMEM((2 * WINDOW, DH), BF16)] * 2,
        ),
        out_shape=jax.ShapeDtypeStruct((blocks, WINDOW, width), F32),
        cost_estimate=attention_cost(blocks, heads),
        name="near_attention",
    )(place, queries, near_keys, near_values, key_rows, value_rows)


def query_kernel(rows, query_ref, packed_ref, near_ref, local_ref, out_ref, flat):
    load_packed(packed_ref, flat, rows)
    gate, up = flat[:DH, :].astype(BF16), flat[DH : 2 * DH, :].astype(BF16)
    down = flat[2 * DH :, :].astype(BF16)
    for at in range(query_ref.shape[0] // WINDOW):
        piece = slice(at * WINDOW, (at + 1) * WINDOW)
        query = query_ref[piece, :]
        pre_gate = dot(query, gate, NT)
        hidden = (pre_gate * jax.nn.sigmoid(pre_gate) * dot(query, up, NT)).astype(BF16)
        fast = dot(hidden, down, NT)
        fast = fast / row_scale(fast)
        out_ref[piece, :] = (fast + (near_ref if at == 0 else local_ref)[...]).astype(BF16)


def query_heads(block_at, queries, packed, near, local, rows):
    _, tokens, width = queries.shape
    heads = width // DH
    shards, padded, _ = packed.shape
    piece = pl.BlockSpec((None, WINDOW, DH), lambda h: (block_at, 0, h))
    return pl.pallas_call(
        functools.partial(query_kernel, rows),
        grid=(heads,),
        in_specs=[
            pl.BlockSpec((None, tokens, DH), lambda h: (block_at, 0, h)),
            pl.BlockSpec((shards // heads, padded, DH), lambda h: (h, 0, 0)),
            piece,
            piece,
        ],
        out_specs=pl.BlockSpec((tokens, DH), lambda h: (0, h)),
        out_shape=jax.ShapeDtypeStruct((tokens, width), BF16),
        scratch_shapes=[pltpu.VMEM((3 * DH, DH), F32)],
        cost_estimate=cost(heads * 6 * tokens * DH * DH, 7e6, heads * tokens * DH),
        name="query_heads",
    )(queries, packed, near, local)


def output_kernel(side_ref, own_ref, other_ref, own_weight, other_weight, *refs):
    out_ref = refs[-1]
    total = dot(own_ref[...], own_weight[...], NN) + dot(other_ref[...], other_weight[...], NN)
    out_ref[...] = total.astype(BF16)


def output(block_at, blocks, side, own, other, weight, other_weight, into):
    tokens, width = own.shape
    tile = 256
    heads = pl.BlockSpec((tile, width), lambda t, side: (t, 0))
    operands = [side, own, other, weight, other_weight] + ([] if into is None else [into])
    return pl.pallas_call(
        output_kernel,
        grid_spec=pltpu.PrefetchScalarGridSpec(
            num_scalar_prefetch=1,
            grid=(tokens // tile,),
            in_specs=[
                heads,
                heads,
                pl.BlockSpec((width, width), lambda t, side: (0, side[0])),
                pl.BlockSpec((width, width), lambda t, side: (0, 0)),
            ]
            + ([] if into is None else [pl.BlockSpec(memory_space=pl.ANY)]),
            out_specs=pl.BlockSpec((None, tile, width), lambda t, side: (block_at, t, 0)),
        ),
        out_shape=jax.ShapeDtypeStruct((blocks, tokens, width), BF16),
        input_output_aliases={} if into is None else {5: 0},
        cost_estimate=cost(4 * tokens * width * width, 6e6),
        name="output",
    )(*operands)


def shards(queries, key_rows, value_rows, step_rates, gate_init, up_init, down_init, out_weight):
    blocks, tokens, width = queries.shape
    heads = width // DH
    count = lax.axis_size("tok")
    place = lax.axis_index("tok")
    side = lax.axis_index("head")
    ring = [(i, (i + 1) % count) for i in range(count)]
    swap = [(0, 1), (1, 0)]
    rows = heads * 3 * DH // count
    padded = -(-(rows + 2) // 8) * 8

    near_keys = lax.ppermute(key_rows[:, tokens - WINDOW :, :], "tok", ring)
    near_values = lax.ppermute(value_rows[:, tokens - WINDOW :, :], "tok", ring)
    sent_weight = lax.dynamic_slice_in_dim(out_weight, (1 - side) * width, width, 1)
    other_weight = lax.ppermute(sent_weight, "head", swap)

    exchange = lambda x: lax.all_to_all(x, "tok", split_axis=0, concat_axis=0, tiled=True)
    flat = jnp.concatenate([gate_init, up_init, down_init], axis=1).reshape(heads * 3 * DH, DH)
    flat = jnp.concatenate([flat, jnp.zeros((padded - rows, DH), F32)], axis=0)
    held = lax.dynamic_slice_in_dim(flat, place * rows, padded, 0)

    local = local_attention(queries, key_rows, value_rows)
    near = near_attention(
        place.reshape(1), queries, near_keys, near_values, key_rows, value_rows
    )
    weights = (gate_init, up_init, down_init)
    result = None
    for block_at in range(blocks):
        parts = gradients(
            block_at, key_rows, value_rows, step_rates, weights, count, rows, padded
        )
        held, copies = update(exchange(parts), held, rows)
        packed = exchange(copies)
        weights = (packed,)
        own = query_heads(block_at, queries, packed, near, local, rows)
        other = lax.ppermute(own, "head", swap)
        result = output(
            block_at, blocks, side.reshape(1), own, other, out_weight, other_weight, result
        )
    return result


def solution(mesh):
    in_specs = (
        P(None, "tok", "head"),
        P(None, "tok", "head"),
        P(None, "tok", "head"),
        P("head", None, "tok"),
        P("head", None, None),
        P("head", None, None),
        P("head", None, None),
        P("head", None),
    )
    out_specs = P(None, "tok", "head")
    return jax.shard_map(shards, mesh=mesh, in_specs=in_specs, out_specs=out_specs, check_vma=False)
```

```python
import functools
import math

import jax
import jax.numpy as jnp
from jax import lax
from jax.experimental import pallas as pl
from jax.experimental.pallas import tpu as pltpu
from jax.sharding import PartitionSpec as P


DH = 384
WINDOW = 384
EPSILON = 1e-06
BF16 = jnp.bfloat16
F32 = jnp.float32
TOKENS_AT_ONCE = 256
QUERY_TILE = 128

NT = (((1,), (1,)), ((), ()))
NN = (((1,), (0,)), ((), ()))


def dot(a, b, dims):
    return lax.dot_general(a, b, dims, preferred_element_type=F32)


def cost(flops, bytes_accessed, transcendentals=0):
    return pl.CostEstimate(
        flops=int(flops), bytes_accessed=int(bytes_accessed), transcendentals=int(transcendentals)
    )


def load_packed(packed_ref, flat, rows):
    for at in range(packed_ref.shape[0]):
        flat[at * rows : (at + 1) * rows, :] = packed_ref[at, :rows, :].astype(F32)


def gradient_kernel(first, block_at, rows, *refs):
    if first:
        key_ref, value_ref, rate_ref, gate_ref, up_ref, down_ref, out_ref, flat, sums = refs
        gate, up = gate_ref[...].astype(BF16), up_ref[...].astype(BF16)
        down_t = jnp.transpose(down_ref[...]).astype(BF16)
    else:
        key_ref, value_ref, rate_ref, packed_ref, out_ref, flat, sums = refs
        load_packed(packed_ref, flat, rows)
        gate, up = flat[:DH, :].astype(BF16), flat[DH : 2 * DH, :].astype(BF16)
        down_t = jnp.transpose(flat[2 * DH :, :]).astype(BF16)
    tokens = key_ref.shape[0]
    rates = rate_ref[block_at : block_at + 1, :]
    for at in range(tokens // TOKENS_AT_ONCE):
        piece = slice(at * TOKENS_AT_ONCE, (at + 1) * TOKENS_AT_ONCE)
        key, value = key_ref[piece, :], value_ref[piece, :]
        rate = rates[:, piece]
        pre_gate = dot(gate, key, NT)
        pre_up = dot(up, key, NT)
        backed = dot(down_t, value, NT) * rate
        sigmoid = jax.nn.sigmoid(pre_gate)
        active = pre_gate * sigmoid
        hidden = (active * pre_up * rate).astype(BF16)
        to_up = (backed * active).astype(BF16)
        slope = sigmoid * (1.0 + pre_gate * (1.0 - sigmoid))
        to_gate = (backed * pre_up * slope).astype(BF16)
        for which, (left, right) in enumerate(((to_gate, key), (to_up, key), (hidden, value))):
            term = dot(left, right, NN)
            if at == 0:
                sums[which] = term
            else:
                sums[which] += term
    flat[:DH, :] = sums[0]
    flat[DH : 2 * DH, :] = sums[1]
    flat[2 * DH :, :] = jnp.transpose(sums[2])
    total = jnp.sum(rates, axis=1, keepdims=True)
    high = total.astype(BF16)
    low = (total - high.astype(F32)).astype(BF16)
    extra = out_ref.shape[1] - rows
    place = lax.broadcasted_iota(jnp.int32, (extra, DH), 0)
    tail = jnp.where(place == 0, high.astype(F32), jnp.where(place == 1, low.astype(F32), 0.0))
    for at in range(out_ref.shape[0]):
        piece = jnp.concatenate([flat[at * rows : (at + 1) * rows, :], tail], axis=0)
        out_ref[at] = piece.astype(BF16)


def gradients(block_at, key_rows, value_rows, step_rates, weights, shards, rows, padded):
    _, tokens, width = key_rows.shape
    heads = width // DH
    first = len(weights) == 3
    matrix = pl.BlockSpec((None, DH, DH), lambda h: (h, 0, 0))
    per_head = shards // heads
    packed = pl.BlockSpec((per_head, padded, DH), lambda h: (h, 0, 0))
    rowed = pl.BlockSpec((None, tokens, DH), lambda h: (block_at, 0, h))
    return pl.pallas_call(
        functools.partial(gradient_kernel, first, block_at, rows),
        grid=(heads,),
        in_specs=[rowed, rowed, pl.BlockSpec((None, step_rates.shape[1], tokens), lambda h: (h, 0, 0))]
        + ([matrix] * 3 if first else [packed]),
        out_specs=packed,
        out_shape=jax.ShapeDtypeStruct((shards, padded, DH), BF16),
        scratch_shapes=[pltpu.VMEM((3 * DH, DH), F32), pltpu.VMEM((3, DH, DH), F32)],
        cost_estimate=cost(heads * 12 * tokens * DH * DH, 8e6, heads * tokens * DH * 2),
        name="gradients",
    )(key_rows, value_rows, step_rates, *weights)


def row_scale(matrix):
    return jnp.sqrt(jnp.mean(matrix * matrix, axis=-1, keepdims=True) + EPSILON)


def update_kernel(rows, parts_ref, old_ref, new_ref, copies_ref):
    total = parts_ref[0].astype(F32)
    for at in range(1, parts_ref.shape[0]):
        total += parts_ref[at].astype(F32)
    rate = total[rows : rows + 1, :] + total[rows + 1 : rows + 2, :]
    old = old_ref[...]
    updated = old + total / rate
    new = updated * (row_scale(old) / row_scale(updated))
    new_ref[...] = new
    rounded = new.astype(BF16)
    for at in range(copies_ref.shape[0]):
        copies_ref[at] = rounded


def update(parts, old, rows):
    shards, padded, _ = parts.shape
    return pl.pallas_call(
        functools.partial(update_kernel, rows),
        out_shape=(
            jax.ShapeDtypeStruct((padded, DH), F32),
            jax.ShapeDtypeStruct((shards, padded, DH), BF16),
        ),
        in_specs=[pl.BlockSpec(memory_space=pltpu.VMEM)] * 2,
        out_specs=(pl.BlockSpec(memory_space=pltpu.VMEM),) * 2,
        compiler_params=pltpu.CompilerParams(vmem_limit_bytes=32 * 2**20),
        cost_estimate=cost(2 * shards * padded * DH, 4e6),
        name="update",
    )(parts, old)


def attend(query_ref, keys, values, out_ref, barred):
    scale = 1.0 / math.sqrt(DH)
    span = WINDOW + QUERY_TILE
    row = lax.broadcasted_iota(jnp.int32, (QUERY_TILE, span), 0)
    column = lax.broadcasted_iota(jnp.int32, (QUERY_TILE, span), 1)
    window = (column > row) & (column <= row + WINDOW)
    for at in range(query_ref.shape[0] // QUERY_TILE):
        low = at * QUERY_TILE
        scores = dot(query_ref[low : low + QUERY_TILE, :], keys[low : low + span, :], NT) * scale
        allowed = window if barred is None else window & (column + low >= barred)
        scores = jnp.where(allowed, scores, -jnp.inf)
        expos = jnp.exp(scores - jnp.max(scores, axis=1, keepdims=True))
        weights = (expos * (1.0 / jnp.sum(expos, axis=1, keepdims=True))).astype(BF16)
        out_ref[low : low + QUERY_TILE, :] = dot(weights, values[low : low + span, :], NN)


def local_kernel(query_ref, key_ref, value_ref, out_ref):
    attend(query_ref, key_ref, value_ref, out_ref, None)


def attention_cost(blocks, heads):
    pairs = blocks * heads * WINDOW * (WINDOW + QUERY_TILE)
    return cost(4 * pairs * DH, 10e6, pairs)


def local_attention(queries, key_rows, value_rows):
    blocks, tokens, width = queries.shape
    heads = width // DH
    last = tokens // WINDOW - 1
    return pl.pallas_call(
        local_kernel,
        grid=(blocks, heads),
        in_specs=[
            pl.BlockSpec((None, WINDOW, DH), lambda b, h: (b, last, h)),
            pl.BlockSpec((None, tokens, DH), lambda b, h: (b, 0, h)),
            pl.BlockSpec((None, tokens, DH), lambda b, h: (b, 0, h)),
        ],
        out_specs=pl.BlockSpec((None, WINDOW, DH), lambda b, h: (b, 0, h)),
        out_shape=jax.ShapeDtypeStruct((blocks, WINDOW, width), F32),
        cost_estimate=attention_cost(blocks, heads),
        name="local_attention",
    )(queries, key_rows, value_rows)


def near_kernel(block_at, place_ref, query_ref, key_ref, value_ref, *refs):
    near, (out_ref, keys, values) = refs[:-3], refs[-3:]
    keys[WINDOW:, :] = key_ref[...]
    values[WINDOW:, :] = value_ref[...]
    keys[:WINDOW, :] = near[0][...]
    values[:WINDOW, :] = near[1][...]
    first = place_ref[0] == 0
    barred = None
    if block_at == 0:
        barred = jnp.where(first, WINDOW, 0)
    else:

        @pl.when(first)
        def _():
            keys[:WINDOW, :] = near[2][...]
            values[:WINDOW, :] = near[3][...]

    attend(query_ref, keys, values, out_ref, barred)


def near_attention(block_at, place, queries, key_rows, value_rows, near):
    width = queries.shape[2]
    heads = width // DH
    own = pl.BlockSpec((None, WINDOW, DH), lambda h, place: (block_at, 0, h))
    rows = pl.BlockSpec((WINDOW, DH), lambda h, place: (0, h))
    return pl.pallas_call(
        functools.partial(near_kernel, block_at),
        grid_spec=pltpu.PrefetchScalarGridSpec(
            num_scalar_prefetch=1,
            grid=(heads,),
            in_specs=[own] * 3 + [rows] * len(near),
            out_specs=rows,
            scratch_shapes=[pltpu.VMEM((2 * WINDOW, DH), BF16)] * 2,
        ),
        out_shape=jax.ShapeDtypeStruct((WINDOW, width), F32),
        cost_estimate=attention_cost(1, heads),
        name="near_attention",
    )(place, queries, key_rows, value_rows, *near)


def query_kernel(rows, query_ref, packed_ref, near_ref, local_ref, out_ref, flat):
    load_packed(packed_ref, flat, rows)
    gate, up = flat[:DH, :].astype(BF16), flat[DH : 2 * DH, :].astype(BF16)
    down = flat[2 * DH :, :].astype(BF16)
    for at in range(query_ref.shape[0] // WINDOW):
        piece = slice(at * WINDOW, (at + 1) * WINDOW)
        query = query_ref[piece, :]
        pre_gate = dot(query, gate, NT)
        hidden = (pre_gate * jax.nn.sigmoid(pre_gate) * dot(query, up, NT)).astype(BF16)
        fast = dot(hidden, down, NT)
        fast = fast / row_scale(fast)
        out_ref[piece, :] = (fast + (near_ref if at == 0 else local_ref)[...]).astype(BF16)


def query_heads(block_at, queries, packed, near, local, rows):
    _, tokens, width = queries.shape
    heads = width // DH
    shards, padded, _ = packed.shape
    return pl.pallas_call(
        functools.partial(query_kernel, rows),
        grid=(heads,),
        in_specs=[
            pl.BlockSpec((None, tokens, DH), lambda h: (block_at, 0, h)),
            pl.BlockSpec((shards // heads, padded, DH), lambda h: (h, 0, 0)),
            pl.BlockSpec((WINDOW, DH), lambda h: (0, h)),
            pl.BlockSpec((None, WINDOW, DH), lambda h: (block_at, 0, h)),
        ],
        out_specs=pl.BlockSpec((tokens, DH), lambda h: (0, h)),
        out_shape=jax.ShapeDtypeStruct((tokens, width), BF16),
        scratch_shapes=[pltpu.VMEM((3 * DH, DH), F32)],
        cost_estimate=cost(heads * 6 * tokens * DH * DH, 7e6, heads * tokens * DH),
        name="query_heads",
    )(queries, packed, near, local)


def output_kernel(side_ref, own_ref, other_ref, own_weight, other_weight, *refs):
    out_ref = refs[-1]
    total = dot(own_ref[...], own_weight[...], NN) + dot(other_ref[...], other_weight[...], NN)
    out_ref[...] = total.astype(BF16)


def output(block_at, blocks, side, own, other, weight, other_weight, into):
    tokens, width = own.shape
    tile = 256
    heads = pl.BlockSpec((tile, width), lambda t, side: (t, 0))
    operands = [side, own, other, weight, other_weight] + ([] if into is None else [into])
    return pl.pallas_call(
        output_kernel,
        grid_spec=pltpu.PrefetchScalarGridSpec(
            num_scalar_prefetch=1,
            grid=(tokens // tile,),
            in_specs=[
                heads,
                heads,
                pl.BlockSpec((width, width), lambda t, side: (0, side[0])),
                pl.BlockSpec((width, width), lambda t, side: (0, 0)),
            ]
            + ([] if into is None else [pl.BlockSpec(memory_space=pl.ANY)]),
            out_specs=pl.BlockSpec((None, tile, width), lambda t, side: (block_at, t, 0)),
        ),
        out_shape=jax.ShapeDtypeStruct((blocks, tokens, width), BF16),
        input_output_aliases={} if into is None else {5: 0},
        cost_estimate=cost(4 * tokens * width * width, 6e6),
        name="output",
    )(*operands)


def shards(queries, key_rows, value_rows, step_rates, gate_init, up_init, down_init, out_weight):
    blocks, tokens, width = queries.shape
    heads = width // DH
    count = lax.axis_size("tok")
    place = lax.axis_index("tok")
    side = lax.axis_index("head")
    ring = [(i, (i + 1) % count) for i in range(count)]
    swap = [(0, 1), (1, 0)]
    rows = heads * 3 * DH // count
    padded = -(-(rows + 2) // 8) * 8

    near = []
    for at, array in enumerate((key_rows, value_rows) * blocks):
        near.append(lax.ppermute(array[at // 2, tokens - WINDOW :, :], "tok", ring))
    sent_weight = lax.dynamic_slice_in_dim(out_weight, (1 - side) * width, width, 1)
    other_weight = lax.ppermute(sent_weight, "head", swap)

    exchange = lambda x: lax.all_to_all(x, "tok", split_axis=0, concat_axis=0, tiled=True)
    flat = jnp.concatenate([gate_init, up_init, down_init], axis=1).reshape(heads * 3 * DH, DH)
    flat = jnp.concatenate([flat, jnp.zeros((padded - rows, DH), F32)], axis=0)
    held = lax.dynamic_slice_in_dim(flat, place * rows, padded, 0)

    local = local_attention(queries, key_rows, value_rows)
    nears = []
    for block_at in range(blocks):
        reach = near[2 * block_at : 2 * block_at + 2] + near[: 2 * block_at][-2:]
        nears.append(
            near_attention(block_at, place.reshape(1), queries, key_rows, value_rows, reach)
        )
    weights = (gate_init, up_init, down_init)
    result = None
    for block_at in range(blocks):
        parts = gradients(block_at, key_rows, value_rows, step_rates, weights, count, rows, padded)
        parts = exchange(parts)
        held, copies = update(parts, held, rows)
        packed = exchange(copies)
        weights = (packed,)
        own = query_heads(block_at, queries, packed, nears[block_at], local, rows)
        other = lax.ppermute(own, "head", swap)
        result = output(
            block_at, blocks, side.reshape(1), own, other, out_weight, other_weight, result
        )
    return result


def solution(mesh):
    in_specs = (
        P(None, "tok", "head"),
        P(None, "tok", "head"),
        P(None, "tok", "head"),
        P("head", None, "tok"),
        P("head", None, None),
        P("head", None, None),
        P("head", None, None),
        P("head", None),
    )
    out_specs = P(None, "tok", "head")
    return jax.shard_map(shards, mesh=mesh, in_specs=in_specs, out_specs=out_specs, check_vma=False)
```

```python
import functools
import math

import jax
import jax.numpy as jnp
from jax import lax
from jax.experimental import pallas as pl
from jax.experimental.pallas import tpu as pltpu
from jax.sharding import PartitionSpec as P


DH = 384
WINDOW = 384
EPSILON = 1e-06
BF16 = jnp.bfloat16
F32 = jnp.float32
TOKENS_AT_ONCE = 256
LEAN = pltpu.CompilerParams(vmem_limit_bytes=36 * 2**20)
QUERY_TILE = 128

NT = (((1,), (1,)), ((), ()))
NN = (((1,), (0,)), ((), ()))


def dot(a, b, dims):
    return lax.dot_general(a, b, dims, preferred_element_type=F32)


def cost(flops, bytes_accessed, transcendentals=0):
    return pl.CostEstimate(
        flops=int(flops), bytes_accessed=int(bytes_accessed), transcendentals=int(transcendentals)
    )


def load_packed(packed_ref, flat, rows):
    for at in range(packed_ref.shape[0]):
        flat[at * rows : (at + 1) * rows, :] = packed_ref[at, :rows, :].astype(F32)


def gradient_kernel(first, block_at, rows, *refs):
    if first:
        key_ref, value_ref, rate_ref, gate_ref, up_ref, down_ref, out_ref, flat, sums = refs
        gate, up = gate_ref[...].astype(BF16), up_ref[...].astype(BF16)
        down_t = jnp.transpose(down_ref[...]).astype(BF16)
    else:
        key_ref, value_ref, rate_ref, packed_ref, out_ref, flat, sums = refs
        load_packed(packed_ref, flat, rows)
        gate, up = flat[:DH, :].astype(BF16), flat[DH : 2 * DH, :].astype(BF16)
        down_t = jnp.transpose(flat[2 * DH :, :]).astype(BF16)
    tokens = key_ref.shape[0]
    rates = rate_ref[block_at : block_at + 1, :]
    for at in range(tokens // TOKENS_AT_ONCE):
        piece = slice(at * TOKENS_AT_ONCE, (at + 1) * TOKENS_AT_ONCE)
        key, value = key_ref[piece, :], value_ref[piece, :]
        rate = rates[:, piece]
        pre_gate = dot(gate, key, NT)
        pre_up = dot(up, key, NT)
        backed = dot(down_t, value, NT) * rate
        sigmoid = jax.nn.sigmoid(pre_gate)
        active = pre_gate * sigmoid
        hidden = (active * pre_up * rate).astype(BF16)
        to_up = (backed * active).astype(BF16)
        slope = sigmoid * (1.0 + pre_gate * (1.0 - sigmoid))
        to_gate = (backed * pre_up * slope).astype(BF16)
        for which, (left, right) in enumerate(((to_gate, key), (to_up, key), (hidden, value))):
            term = dot(left, right, NN)
            if at == 0:
                sums[which] = term
            else:
                sums[which] += term
    flat[:DH, :] = sums[0]
    flat[DH : 2 * DH, :] = sums[1]
    flat[2 * DH :, :] = jnp.transpose(sums[2])
    total = jnp.sum(rates, axis=1, keepdims=True)
    high = total.astype(BF16)
    low = (total - high.astype(F32)).astype(BF16)
    extra = out_ref.shape[1] - rows
    place = lax.broadcasted_iota(jnp.int32, (extra, DH), 0)
    tail = jnp.where(place == 0, high.astype(F32), jnp.where(place == 1, low.astype(F32), 0.0))
    for at in range(out_ref.shape[0]):
        piece = jnp.concatenate([flat[at * rows : (at + 1) * rows, :], tail], axis=0)
        out_ref[at] = piece.astype(BF16)


def gradients(block_at, key_rows, value_rows, step_rates, weights, shards, rows, padded):
    _, tokens, width = key_rows.shape
    heads = width // DH
    first = len(weights) == 3
    matrix = pl.BlockSpec((None, DH, DH), lambda h: (h, 0, 0))
    per_head = shards // heads
    packed = pl.BlockSpec((per_head, padded, DH), lambda h: (h, 0, 0))
    rowed = pl.BlockSpec((None, tokens, DH), lambda h: (block_at, 0, h))
    return pl.pallas_call(
        functools.partial(gradient_kernel, first, block_at, rows),
        grid=(heads,),
        in_specs=[rowed, rowed, pl.BlockSpec((None, step_rates.shape[1], tokens), lambda h: (h, 0, 0))]
        + ([matrix] * 3 if first else [packed]),
        out_specs=packed,
        out_shape=jax.ShapeDtypeStruct((shards, padded, DH), BF16),
        scratch_shapes=[pltpu.VMEM((3 * DH, DH), F32), pltpu.VMEM((3, DH, DH), F32)],
        cost_estimate=cost(heads * 12 * tokens * DH * DH, 8e6, heads * tokens * DH * 2),
        name="gradients",
    )(key_rows, value_rows, step_rates, *weights)


def row_scale(matrix):
    return jnp.sqrt(jnp.mean(matrix * matrix, axis=-1, keepdims=True) + EPSILON)


def update_kernel(rows, parts_ref, old_ref, new_ref, copies_ref):
    total = parts_ref[0].astype(F32)
    for at in range(1, parts_ref.shape[0]):
        total += parts_ref[at].astype(F32)
    rate = total[rows : rows + 1, :] + total[rows + 1 : rows + 2, :]
    old = old_ref[...]
    updated = old + total / rate
    new = updated * (row_scale(old) / row_scale(updated))
    new_ref[...] = new
    rounded = new.astype(BF16)
    for at in range(copies_ref.shape[0]):
        copies_ref[at] = rounded


def update(parts, old, rows):
    shards, padded, _ = parts.shape
    return pl.pallas_call(
        functools.partial(update_kernel, rows),
        out_shape=(
            jax.ShapeDtypeStruct((padded, DH), F32),
            jax.ShapeDtypeStruct((shards, padded, DH), BF16),
        ),
        in_specs=[pl.BlockSpec(memory_space=pltpu.VMEM)] * 2,
        out_specs=(pl.BlockSpec(memory_space=pltpu.VMEM),) * 2,
        compiler_params=LEAN,
        cost_estimate=cost(2 * shards * padded * DH, 4e6),
        name="update",
    )(parts, old)


def attend(query_ref, keys, values, out_ref, barred):
    scale = 1.0 / math.sqrt(DH)
    span = WINDOW + QUERY_TILE
    row = lax.broadcasted_iota(jnp.int32, (QUERY_TILE, span), 0)
    column = lax.broadcasted_iota(jnp.int32, (QUERY_TILE, span), 1)
    window = (column > row) & (column <= row + WINDOW)
    for at in range(query_ref.shape[0] // QUERY_TILE):
        low = at * QUERY_TILE
        scores = dot(query_ref[low : low + QUERY_TILE, :], keys[low : low + span, :], NT) * scale
        allowed = window if barred is None else window & (column + low >= barred)
        scores = jnp.where(allowed, scores, -jnp.inf)
        expos = jnp.exp(scores - jnp.max(scores, axis=1, keepdims=True))
        weights = (expos * (1.0 / jnp.sum(expos, axis=1, keepdims=True))).astype(BF16)
        mixed = dot(weights, values[low : low + span, :], NN)
        out_ref[low : low + QUERY_TILE, :] = mixed.astype(BF16)


def local_kernel(query_ref, key_ref, value_ref, out_ref):
    attend(query_ref, key_ref, value_ref, out_ref, None)


def attention_cost(blocks, heads):
    pairs = blocks * heads * WINDOW * (WINDOW + QUERY_TILE)
    return cost(4 * pairs * DH, 10e6, pairs)


def local_attention(queries, key_rows, value_rows):
    blocks, tokens, width = queries.shape
    heads = width // DH
    last = tokens // WINDOW - 1
    return pl.pallas_call(
        local_kernel,
        grid=(blocks, heads),
        in_specs=[
            pl.BlockSpec((None, WINDOW, DH), lambda b, h: (b, last, h)),
            pl.BlockSpec((None, tokens, DH), lambda b, h: (b, 0, h)),
            pl.BlockSpec((None, tokens, DH), lambda b, h: (b, 0, h)),
        ],
        out_specs=pl.BlockSpec((None, WINDOW, DH), lambda b, h: (b, 0, h)),
        out_shape=jax.ShapeDtypeStruct((blocks, WINDOW, width), BF16),
        cost_estimate=attention_cost(blocks, heads),
        name="local_attention",
    )(queries, key_rows, value_rows)


def near_kernel(block_at, place_ref, query_ref, key_ref, value_ref, *refs):
    near, (out_ref, keys, values) = refs[:-3], refs[-3:]
    keys[WINDOW:, :] = key_ref[...]
    values[WINDOW:, :] = value_ref[...]
    keys[:WINDOW, :] = near[0][...]
    values[:WINDOW, :] = near[1][...]
    first = place_ref[0] == 0
    barred = None
    if block_at == 0:
        barred = jnp.where(first, WINDOW, 0)
    else:

        @pl.when(first)
        def _():
            keys[:WINDOW, :] = near[2][...]
            values[:WINDOW, :] = near[3][...]

    attend(query_ref, keys, values, out_ref, barred)


def near_attention(block_at, place, queries, key_rows, value_rows, near):
    width = queries.shape[2]
    heads = width // DH
    own = pl.BlockSpec((None, WINDOW, DH), lambda h, place: (block_at, 0, h))
    rows = pl.BlockSpec((WINDOW, DH), lambda h, place: (0, h))
    return pl.pallas_call(
        functools.partial(near_kernel, block_at),
        grid_spec=pltpu.PrefetchScalarGridSpec(
            num_scalar_prefetch=1,
            grid=(heads,),
            in_specs=[own] * 3 + [rows] * len(near),
            out_specs=rows,
            scratch_shapes=[pltpu.VMEM((2 * WINDOW, DH), BF16)] * 2,
        ),
        out_shape=jax.ShapeDtypeStruct((WINDOW, width), BF16),
        cost_estimate=attention_cost(1, heads),
        name="near_attention",
    )(place, queries, key_rows, value_rows, *near)


def query_kernel(rows, query_ref, packed_ref, near_ref, local_ref, out_ref, flat):
    load_packed(packed_ref, flat, rows)
    gate, up = flat[:DH, :].astype(BF16), flat[DH : 2 * DH, :].astype(BF16)
    down = flat[2 * DH :, :].astype(BF16)
    for at in range(query_ref.shape[0] // WINDOW):
        piece = slice(at * WINDOW, (at + 1) * WINDOW)
        query = query_ref[piece, :]
        pre_gate = dot(query, gate, NT)
        hidden = (pre_gate * jax.nn.sigmoid(pre_gate) * dot(query, up, NT)).astype(BF16)
        fast = dot(hidden, down, NT)
        fast = fast / row_scale(fast)
        attended = (near_ref if at == 0 else local_ref)[...].astype(F32)
        out_ref[piece, :] = (fast + attended).astype(BF16)


def query_heads(block_at, first, heads, queries, packed, near, local, rows, params):
    _, tokens, width = queries.shape
    shards, padded, _ = packed.shape
    per_head = shards * DH // width
    return pl.pallas_call(
        functools.partial(query_kernel, rows),
        grid=(heads,),
        in_specs=[
            pl.BlockSpec((None, tokens, DH), lambda h: (block_at, 0, first + h)),
            pl.BlockSpec((per_head, padded, DH), lambda h: (first + h, 0, 0)),
            pl.BlockSpec((WINDOW, DH), lambda h: (0, first + h)),
            pl.BlockSpec((None, WINDOW, DH), lambda h: (block_at, 0, first + h)),
        ],
        out_specs=pl.BlockSpec((tokens, DH), lambda h: (0, h)),
        out_shape=jax.ShapeDtypeStruct((tokens, heads * DH), BF16),
        scratch_shapes=[pltpu.VMEM((3 * DH, DH), F32)],
        compiler_params=params,
        cost_estimate=cost(heads * 6 * tokens * DH * DH, heads * 3.5e6, heads * tokens * DH),
        name="query_heads",
    )(queries, packed, near, local)


def project_kernel(terms, has_sum, side_ref, *refs):
    out_ref = refs[-1]
    total = refs[2 * terms][...] if has_sum else None
    for at in range(terms):
        term = dot(refs[2 * at][...], refs[2 * at + 1][...], NN)
        total = term if total is None else total + term
    out_ref[...] = total.astype(out_ref.dtype)


def project(side, terms, tokens, summed=None, into=None, block_at=0, blocks=0, params=None):
    tile = 256
    specs, operands = [], []
    columns = terms[0][1].shape[0]
    for array, weight, first, own in terms:
        depth = array.shape[1]
        operands += [array, weight]
        specs.append(pl.BlockSpec((tile, depth), lambda t, side: (t, 0)))
        specs.append(
            pl.BlockSpec(
                (depth, columns),
                lambda t, side, first=first, own=own: (first, side[0] if own else 0),
            )
        )
    if summed is not None:
        operands.append(summed)
        specs.append(pl.BlockSpec((tile, columns), lambda t, side: (t, 0)))
    if into is not None:
        operands.append(into)
        specs.append(pl.BlockSpec(memory_space=pl.ANY))
    if blocks:
        out_spec = pl.BlockSpec((None, tile, columns), lambda t, side: (block_at, t, 0))
        out_shape = jax.ShapeDtypeStruct((blocks, tokens, columns), BF16)
    else:
        out_spec = pl.BlockSpec((tile, columns), lambda t, side: (t, 0))
        out_shape = jax.ShapeDtypeStruct((tokens, columns), F32)
    depth = sum(term[0].shape[1] for term in terms)
    return pl.pallas_call(
        functools.partial(project_kernel, len(terms), summed is not None),
        grid_spec=pltpu.PrefetchScalarGridSpec(
            num_scalar_prefetch=1, grid=(tokens // tile,), in_specs=specs, out_specs=out_spec
        ),
        out_shape=out_shape,
        input_output_aliases={} if into is None else {len(operands): 0},
        compiler_params=params,
        cost_estimate=cost(2 * tokens * columns * depth, 6e6),
        name="project",
    )(side, *operands)


def exchange_order(count):
    side = round(count ** (1 / 3))
    if side**3 != count:
        return list(range(count))
    order = []
    for step in range(count):
        a, b, c = step // (side * side), step // side % side, step % side
        x, y, z = a, b, c
        order.append((x * side + y) * side + z)
    return order


def shards(queries, key_rows, value_rows, step_rates, gate_init, up_init, down_init, out_weight):
    blocks, tokens, width = queries.shape
    heads = width // DH
    count = lax.axis_size("tok")
    place = lax.axis_index("tok")
    side = lax.axis_index("head")
    ring = [(i, (i + 1) % count) for i in range(count)]
    swap = [(0, 1), (1, 0)]
    rows = heads * 3 * DH // count
    padded = -(-(rows + 2) // 8) * 8

    weights = (gate_init, up_init, down_init)
    near = [lax.ppermute(key_rows[0, tokens - WINDOW :, :], "tok", ring)]
    parts = gradients(0, key_rows, value_rows, step_rates, weights, count, rows, padded)
    later_keys, later_values, parts = lax.optimization_barrier((key_rows, value_rows, parts))
    for at, array in enumerate((later_keys, later_values) * blocks):
        if at:
            near.append(lax.ppermute(array[at // 2, tokens - WINDOW :, :], "tok", ring))
    sent_weight = lax.dynamic_slice_in_dim(out_weight, (1 - side) * width, width, 1)
    other_weight = lax.ppermute(sent_weight, "head", swap)

    order = exchange_order(count)
    exchange = lambda x: lax.all_to_all(
        x, "tok", split_axis=0, concat_axis=0, tiled=True, axis_index_groups=[order]
    )
    flat = jnp.concatenate([gate_init, up_init, down_init], axis=1).reshape(heads * 3 * DH, DH)
    flat = jnp.concatenate([flat, jnp.zeros((padded - rows, DH), F32)], axis=0)
    shard = jnp.asarray([order.index(i) for i in range(count)], jnp.int32)[place]
    held = lax.dynamic_slice_in_dim(flat, shard * rows, padded, 0)

    local = local_attention(queries, key_rows, value_rows)
    nears = []
    for block_at in range(blocks):
        reach = near[2 * block_at : 2 * block_at + 2] + near[: 2 * block_at][-2:]
        nears.append(
            near_attention(block_at, place.reshape(1), queries, key_rows, value_rows, reach)
        )
    result = None
    side_ref = side.reshape(1)
    for block_at in range(blocks):
        last = block_at == blocks - 1
        parts = exchange(parts)
        held, copies = update(parts, held, rows)
        packed = exchange(copies)
        near_now = nears[block_at]
        if not last:
            parts = gradients(
                block_at + 1, key_rows, value_rows, step_rates, (packed,), count, rows, padded
            )
            own = query_heads(
                block_at, 0, heads, queries, packed, near_now, local, rows, None
            )
            other = lax.ppermute(own, "head", swap)
            terms = [(own, out_weight, 0, True), (other, other_weight, 0, False)]
            result = project(side_ref, terms, tokens, None, result, block_at, blocks)
            continue
        own = query_heads(block_at, 0, heads, queries, packed, near_now, local, rows, None)
        other = lax.ppermute(own, "head", swap)
        terms = [(own, out_weight, 0, True), (other, other_weight, 0, False)]
        result = project(side_ref, terms, tokens, None, result, block_at, blocks, LEAN)
    return result


def solution(mesh):
    in_specs = (
        P(None, "tok", "head"),
        P(None, "tok", "head"),
        P(None, "tok", "head"),
        P("head", None, "tok"),
        P("head", None, None),
        P("head", None, None),
        P("head", None, None),
        P("head", None),
    )
    out_specs = P(None, "tok", "head")
    return jax.shard_map(shards, mesh=mesh, in_specs=in_specs, out_specs=out_specs, check_vma=False)
```

```python
import functools
import math

import jax
import jax.numpy as jnp
from jax import lax
from jax.experimental import pallas as pl
from jax.experimental.pallas import tpu as pltpu
from jax.sharding import PartitionSpec as P


DH = 384
WINDOW = 384
EPSILON = 1e-06
BF16 = jnp.bfloat16
F32 = jnp.float32
LANES = 128
PARTS = DH // LANES
LEAN = pltpu.CompilerParams(vmem_limit_bytes=36 * 2**20)
QUERY_TILE = 128

NT = (((1,), (1,)), ((), ()))
NN = (((1,), (0,)), ((), ()))


def dot(a, b, dims):
    return lax.dot_general(a, b, dims, preferred_element_type=F32)


def cost(flops, bytes_accessed, transcendentals=0):
    return pl.CostEstimate(
        flops=int(flops), bytes_accessed=int(bytes_accessed), transcendentals=int(transcendentals)
    )


def load_packed(packed_ref, flat, rows):
    for at in range(packed_ref.shape[0]):
        shard = packed_ref[at].astype(F32)
        for part in range(PARTS):
            columns = slice(part * LANES, (part + 1) * LANES)
            flat[at * rows : (at + 1) * rows, columns] = shard[part * rows : (part + 1) * rows, :]


def gradient_kernel(first, block_at, rows, *refs):
    if first:
        key_ref, value_ref, rate_ref, gate_ref, up_ref, down_ref, out_ref, flat = refs
        gate, up = gate_ref[...].astype(BF16), up_ref[...].astype(BF16)
        down_t = jnp.transpose(down_ref[...]).astype(BF16)
    else:
        key_ref, value_ref, rate_ref, packed_ref, out_ref, flat = refs
        load_packed(packed_ref, flat, rows)
        gate, up = flat[:DH, :].astype(BF16), flat[DH : 2 * DH, :].astype(BF16)
        down_t = jnp.transpose(flat[2 * DH :, :]).astype(BF16)
    key, value = key_ref[...], value_ref[...]
    rate = rate_ref[block_at : block_at + 1, :]
    pre_gate = dot(gate, key, NT)
    pre_up = dot(up, key, NT)
    backed = dot(down_t, value, NT) * rate
    sigmoid = jax.nn.sigmoid(pre_gate)
    active = pre_gate * sigmoid
    hidden = (active * pre_up * rate).astype(BF16)
    to_up = (backed * active).astype(BF16)
    slope = sigmoid * (1.0 + pre_gate * (1.0 - sigmoid))
    to_gate = (backed * pre_up * slope).astype(BF16)
    flat[:DH, :] = dot(to_gate, key, NN)
    flat[DH : 2 * DH, :] = dot(to_up, key, NN)
    flat[2 * DH :, :] = jnp.transpose(dot(hidden, value, NN))
    total = jnp.sum(rate, axis=1, keepdims=True)
    high = total.astype(BF16)
    low = (total - high.astype(F32)).astype(BF16)
    extra = out_ref.shape[1] - PARTS * rows
    place = lax.broadcasted_iota(jnp.int32, (extra, LANES), 0)
    tail = jnp.where(place == 0, high.astype(F32), jnp.where(place == 1, low.astype(F32), 0.0))
    for at in range(out_ref.shape[0]):
        shard = [
            flat[at * rows : (at + 1) * rows, part * LANES : (part + 1) * LANES]
            for part in range(PARTS)
        ]
        out_ref[at] = jnp.concatenate(shard + [tail], axis=0).astype(BF16)


def gradients(block_at, key_rows, value_rows, step_rates, weights, shards, rows, padded):
    _, tokens, width = key_rows.shape
    heads = width // DH
    first = len(weights) == 3
    matrix = pl.BlockSpec((None, DH, DH), lambda h: (h, 0, 0))
    per_head = shards // heads
    packed = pl.BlockSpec((per_head, padded, LANES), lambda h: (h, 0, 0))
    rowed = pl.BlockSpec((None, tokens, DH), lambda h: (block_at, 0, h))
    return pl.pallas_call(
        functools.partial(gradient_kernel, first, block_at, rows),
        grid=(heads,),
        in_specs=[rowed, rowed, pl.BlockSpec((None, step_rates.shape[1], tokens), lambda h: (h, 0, 0))]
        + ([matrix] * 3 if first else [packed]),
        out_specs=packed,
        out_shape=jax.ShapeDtypeStruct((shards, padded, LANES), BF16),
        scratch_shapes=[pltpu.VMEM((3 * DH, DH), F32)],
        cost_estimate=cost(heads * 12 * tokens * DH * DH, 8e6, heads * tokens * DH * 2),
        name="gradients",
    )(key_rows, value_rows, step_rates, *weights)


def row_scale(matrix):
    return jnp.sqrt(jnp.mean(matrix * matrix, axis=-1, keepdims=True) + EPSILON)


def shard_scale(shard, rows):
    square = jnp.sum(shard * shard, axis=-1, keepdims=True)
    total = sum(square[part * rows : (part + 1) * rows] for part in range(PARTS))
    return jnp.sqrt(total / DH + EPSILON)


def update_kernel(rows, parts_ref, old_ref, new_ref, copies_ref):
    total = parts_ref[0].astype(F32)
    for at in range(1, parts_ref.shape[0]):
        total += parts_ref[at].astype(F32)
    top = PARTS * rows
    rate = total[top : top + 1, :] + total[top + 1 : top + 2, :]
    old = old_ref[...]
    updated = old + total / rate
    ratio = shard_scale(old, rows) / shard_scale(updated, rows)
    rest = jnp.ones((old.shape[0] - top, 1), F32)
    new = updated * jnp.concatenate([ratio] * PARTS + [rest], axis=0)
    new_ref[...] = new
    rounded = new.astype(BF16)
    for at in range(copies_ref.shape[0]):
        copies_ref[at] = rounded


def update(parts, old, rows):
    shards, padded, _ = parts.shape
    return pl.pallas_call(
        functools.partial(update_kernel, rows),
        out_shape=(
            jax.ShapeDtypeStruct((padded, LANES), F32),
            jax.ShapeDtypeStruct((shards, padded, LANES), BF16),
        ),
        in_specs=[pl.BlockSpec(memory_space=pltpu.VMEM)] * 2,
        out_specs=(pl.BlockSpec(memory_space=pltpu.VMEM),) * 2,
        compiler_params=LEAN,
        cost_estimate=cost(2 * shards * padded * LANES, 4e6),
        name="update",
    )(parts, old)


def attend(query_ref, keys, values, out_ref, barred):
    scale = 1.0 / math.sqrt(DH)
    span = WINDOW + QUERY_TILE
    row = lax.broadcasted_iota(jnp.int32, (QUERY_TILE, span), 0)
    column = lax.broadcasted_iota(jnp.int32, (QUERY_TILE, span), 1)
    window = (column > row) & (column <= row + WINDOW)
    for at in range(query_ref.shape[0] // QUERY_TILE):
        low = at * QUERY_TILE
        scores = dot(query_ref[low : low + QUERY_TILE, :], keys[low : low + span, :], NT) * scale
        allowed = window if barred is None else window & (column + low >= barred)
        scores = jnp.where(allowed, scores, -jnp.inf)
        expos = jnp.exp(scores - jnp.max(scores, axis=1, keepdims=True))
        weights = (expos * (1.0 / jnp.sum(expos, axis=1, keepdims=True))).astype(BF16)
        mixed = dot(weights, values[low : low + span, :], NN)
        out_ref[low : low + QUERY_TILE, :] = mixed.astype(BF16)


def local_kernel(query_ref, key_ref, value_ref, out_ref):
    attend(query_ref, key_ref, value_ref, out_ref, None)


def attention_cost(blocks, heads):
    pairs = blocks * heads * WINDOW * (WINDOW + QUERY_TILE)
    return cost(4 * pairs * DH, 10e6, pairs)


def local_attention(queries, key_rows, value_rows):
    blocks, tokens, width = queries.shape
    heads = width // DH
    last = tokens // WINDOW - 1
    return pl.pallas_call(
        local_kernel,
        grid=(blocks, heads),
        in_specs=[
            pl.BlockSpec((None, WINDOW, DH), lambda b, h: (b, last, h)),
            pl.BlockSpec((None, tokens, DH), lambda b, h: (b, 0, h)),
            pl.BlockSpec((None, tokens, DH), lambda b, h: (b, 0, h)),
        ],
        out_specs=pl.BlockSpec((None, WINDOW, DH), lambda b, h: (b, 0, h)),
        out_shape=jax.ShapeDtypeStruct((blocks, WINDOW, width), BF16),
        cost_estimate=attention_cost(blocks, heads),
        name="local_attention",
    )(queries, key_rows, value_rows)


def near_kernel(block_at, place_ref, query_ref, key_ref, value_ref, *refs):
    near, (out_ref, keys, values) = refs[:-3], refs[-3:]
    keys[WINDOW:, :] = key_ref[...]
    values[WINDOW:, :] = value_ref[...]
    keys[:WINDOW, :] = near[0][...]
    values[:WINDOW, :] = near[1][...]
    first = place_ref[0] == 0
    barred = None
    if block_at == 0:
        barred = jnp.where(first, WINDOW, 0)
    else:

        @pl.when(first)
        def _():
            keys[:WINDOW, :] = near[2][...]
            values[:WINDOW, :] = near[3][...]

    attend(query_ref, keys, values, out_ref, barred)


def near_attention(block_at, place, queries, key_rows, value_rows, near):
    width = queries.shape[2]
    heads = width // DH
    own = pl.BlockSpec((None, WINDOW, DH), lambda h, place: (block_at, 0, h))
    rows = pl.BlockSpec((WINDOW, DH), lambda h, place: (0, h))
    return pl.pallas_call(
        functools.partial(near_kernel, block_at),
        grid_spec=pltpu.PrefetchScalarGridSpec(
            num_scalar_prefetch=1,
            grid=(heads,),
            in_specs=[own] * 3 + [rows] * len(near),
            out_specs=rows,
            scratch_shapes=[pltpu.VMEM((2 * WINDOW, DH), BF16)] * 2,
        ),
        out_shape=jax.ShapeDtypeStruct((WINDOW, width), BF16),
        cost_estimate=attention_cost(1, heads),
        name="near_attention",
    )(place, queries, key_rows, value_rows, *near)


def query_kernel(rows, query_ref, packed_ref, near_ref, local_ref, out_ref, flat):
    load_packed(packed_ref, flat, rows)
    gate, up = flat[:DH, :].astype(BF16), flat[DH : 2 * DH, :].astype(BF16)
    down = flat[2 * DH :, :].astype(BF16)
    for at in range(query_ref.shape[0] // WINDOW):
        piece = slice(at * WINDOW, (at + 1) * WINDOW)
        query = query_ref[piece, :]
        pre_gate = dot(query, gate, NT)
        hidden = (pre_gate * jax.nn.sigmoid(pre_gate) * dot(query, up, NT)).astype(BF16)
        fast = dot(hidden, down, NT)
        fast = fast / row_scale(fast)
        attended = (near_ref if at == 0 else local_ref)[...].astype(F32)
        out_ref[piece, :] = (fast + attended).astype(BF16)


def query_heads(block_at, first, heads, queries, packed, near, local, rows, params):
    _, tokens, width = queries.shape
    shards, padded, _ = packed.shape
    per_head = shards * DH // width
    return pl.pallas_call(
        functools.partial(query_kernel, rows),
        grid=(heads,),
        in_specs=[
            pl.BlockSpec((None, tokens, DH), lambda h: (block_at, 0, first + h)),
            pl.BlockSpec((per_head, padded, LANES), lambda h: (first + h, 0, 0)),
            pl.BlockSpec((WINDOW, DH), lambda h: (0, first + h)),
            pl.BlockSpec((None, WINDOW, DH), lambda h: (block_at, 0, first + h)),
        ],
        out_specs=pl.BlockSpec((tokens, DH), lambda h: (0, h)),
        out_shape=jax.ShapeDtypeStruct((tokens, heads * DH), BF16),
        scratch_shapes=[pltpu.VMEM((3 * DH, DH), F32)],
        compiler_params=params,
        cost_estimate=cost(heads * 6 * tokens * DH * DH, heads * 3.5e6, heads * tokens * DH),
        name="query_heads",
    )(queries, packed, near, local)


def project_kernel(terms, has_sum, side_ref, *refs):
    out_ref = refs[-1]
    total = refs[2 * terms][...] if has_sum else None
    for at in range(terms):
        term = dot(refs[2 * at][...], refs[2 * at + 1][...], NN)
        total = term if total is None else total + term
    out_ref[...] = total.astype(out_ref.dtype)


def project(side, terms, tokens, summed=None, into=None, block_at=0, blocks=0, params=None):
    tile = 256
    specs, operands = [], []
    columns = terms[0][1].shape[0]
    for array, weight, first, own in terms:
        depth = array.shape[1]
        operands += [array, weight]
        specs.append(pl.BlockSpec((tile, depth), lambda t, side: (t, 0)))
        specs.append(
            pl.BlockSpec(
                (depth, columns),
                lambda t, side, first=first, own=own: (first, side[0] if own else 0),
            )
        )
    if summed is not None:
        operands.append(summed)
        specs.append(pl.BlockSpec((tile, columns), lambda t, side: (t, 0)))
    if into is not None:
        operands.append(into)
        specs.append(pl.BlockSpec(memory_space=pl.ANY))
    if blocks:
        out_spec = pl.BlockSpec((None, tile, columns), lambda t, side: (block_at, t, 0))
        out_shape = jax.ShapeDtypeStruct((blocks, tokens, columns), BF16)
    else:
        out_spec = pl.BlockSpec((tile, columns), lambda t, side: (t, 0))
        out_shape = jax.ShapeDtypeStruct((tokens, columns), F32)
    depth = sum(term[0].shape[1] for term in terms)
    return pl.pallas_call(
        functools.partial(project_kernel, len(terms), summed is not None),
        grid_spec=pltpu.PrefetchScalarGridSpec(
            num_scalar_prefetch=1, grid=(tokens // tile,), in_specs=specs, out_specs=out_spec
        ),
        out_shape=out_shape,
        input_output_aliases={} if into is None else {len(operands): 0},
        compiler_params=params,
        cost_estimate=cost(2 * tokens * columns * depth, 6e6),
        name="project",
    )(side, *operands)


def shards(queries, key_rows, value_rows, step_rates, gate_init, up_init, down_init, out_weight):
    blocks, tokens, width = queries.shape
    heads = width // DH
    count = lax.axis_size("tok")
    place = lax.axis_index("tok")
    side = lax.axis_index("head")
    ring = [(i, (i + 1) % count) for i in range(count)]
    swap = [(0, 1), (1, 0)]
    rows = heads * 3 * DH // count
    padded = -(-(PARTS * rows + 2) // 8) * 8

    weights = (gate_init, up_init, down_init)
    near = [lax.ppermute(key_rows[0, tokens - WINDOW :, :], "tok", ring)]
    parts = gradients(0, key_rows, value_rows, step_rates, weights, count, rows, padded)
    later_keys, later_values, parts = lax.optimization_barrier((key_rows, value_rows, parts))
    for at, array in enumerate((later_keys, later_values) * blocks):
        if at:
            near.append(lax.ppermute(array[at // 2, tokens - WINDOW :, :], "tok", ring))
    sent_weight = lax.dynamic_slice_in_dim(out_weight, (1 - side) * width, width, 1)
    other_weight = lax.ppermute(sent_weight, "head", swap)

    exchange = lambda x: lax.all_to_all(x, "tok", split_axis=0, concat_axis=0, tiled=True)
    flat = jnp.concatenate([gate_init, up_init, down_init], axis=1).reshape(heads * 3 * DH, DH)
    held = lax.dynamic_slice_in_dim(flat, place * rows, rows, 0)
    held = [held[:, part * LANES : (part + 1) * LANES] for part in range(PARTS)]
    held = jnp.concatenate(held + [jnp.zeros((padded - PARTS * rows, LANES), F32)], axis=0)

    local = local_attention(queries, key_rows, value_rows)
    nears = []
    for block_at in range(blocks):
        reach = near[2 * block_at : 2 * block_at + 2] + near[: 2 * block_at][-2:]
        nears.append(
            near_attention(block_at, place.reshape(1), queries, key_rows, value_rows, reach)
        )
    result = None
    side_ref = side.reshape(1)
    for block_at in range(blocks):
        last = block_at == blocks - 1
        parts = exchange(parts)
        held, copies = update(parts, held, rows)
        packed = exchange(copies)
        near_now = nears[block_at]
        if not last:
            parts = gradients(
                block_at + 1, key_rows, value_rows, step_rates, (packed,), count, rows, padded
            )
            own = query_heads(
                block_at, 0, heads, queries, packed, near_now, local, rows, None
            )
            other = lax.ppermute(own, "head", swap)
            terms = [(own, out_weight, 0, True), (other, other_weight, 0, False)]
            result = project(side_ref, terms, tokens, None, result, block_at, blocks)
            continue
        own = query_heads(block_at, 0, heads, queries, packed, near_now, local, rows, None)
        other = lax.ppermute(own, "head", swap)
        terms = [(own, out_weight, 0, True), (other, other_weight, 0, False)]
        result = project(side_ref, terms, tokens, None, result, block_at, blocks, LEAN)
    return result


def solution(mesh):
    in_specs = (
        P(None, "tok", "head"),
        P(None, "tok", "head"),
        P(None, "tok", "head"),
        P("head", None, "tok"),
        P("head", None, None),
        P("head", None, None),
        P("head", None, None),
        P("head", None),
    )
    out_specs = P(None, "tok", "head")
    return jax.shard_map(shards, mesh=mesh, in_specs=in_specs, out_specs=out_specs, check_vma=False)
```

```python
import functools
import math

import jax
import jax.numpy as jnp
from jax import lax
from jax.experimental import pallas as pl
from jax.experimental.pallas import tpu as pltpu
from jax.sharding import PartitionSpec as P


DH = 384
WINDOW = 384
EPSILON = 1e-06
BF16 = jnp.bfloat16
F32 = jnp.float32
LANES = 128
PARTS = DH // LANES
MID = pltpu.CompilerParams(vmem_limit_bytes=48 * 2**20)
LEAN = pltpu.CompilerParams(vmem_limit_bytes=36 * 2**20)
QUERY_TILE = 128

NT = (((1,), (1,)), ((), ()))
NN = (((1,), (0,)), ((), ()))


def dot(a, b, dims):
    return lax.dot_general(a, b, dims, preferred_element_type=F32)


def cost(flops, bytes_accessed, transcendentals=0):
    return pl.CostEstimate(
        flops=int(flops), bytes_accessed=int(bytes_accessed), transcendentals=int(transcendentals)
    )


def load_packed(packed_ref, flat, rows):
    for at in range(packed_ref.shape[0]):
        shard = packed_ref[at].astype(F32)
        for part in range(PARTS):
            columns = slice(part * LANES, (part + 1) * LANES)
            flat[at * rows : (at + 1) * rows, columns] = shard[part * rows : (part + 1) * rows, :]


def in_hbm(array):
    return pltpu.with_memory_space_constraint(array, pltpu.HBM)


def gradient_kernel(first, block_at, rows, *refs):
    if first:
        key_ref, value_ref, rate_ref, gate_ref, up_ref, down_ref, out_ref, flat = refs
        gate, up = gate_ref[...].astype(BF16), up_ref[...].astype(BF16)
        down_t = jnp.transpose(down_ref[...]).astype(BF16)
    else:
        key_ref, value_ref, rate_ref, packed_ref, out_ref, flat = refs
        load_packed(packed_ref, flat, rows)
        gate, up = flat[:DH, :].astype(BF16), flat[DH : 2 * DH, :].astype(BF16)
        down_t = jnp.transpose(flat[2 * DH :, :]).astype(BF16)
    key, value = key_ref[...], value_ref[...]
    rate = rate_ref[block_at : block_at + 1, :]
    pre_gate = dot(gate, key, NT)
    pre_up = dot(up, key, NT)
    backed = dot(down_t, value, NT) * rate
    sigmoid = jax.nn.sigmoid(pre_gate)
    active = pre_gate * sigmoid
    hidden = (active * pre_up * rate).astype(BF16)
    to_up = (backed * active).astype(BF16)
    slope = sigmoid * (1.0 + pre_gate * (1.0 - sigmoid))
    to_gate = (backed * pre_up * slope).astype(BF16)
    flat[:DH, :] = dot(to_gate, key, NN)
    flat[DH : 2 * DH, :] = dot(to_up, key, NN)
    flat[2 * DH :, :] = jnp.transpose(dot(hidden, value, NN))
    total = jnp.sum(rate, axis=1, keepdims=True)
    high = total.astype(BF16)
    low = (total - high.astype(F32)).astype(BF16)
    extra = out_ref.shape[1] - PARTS * rows
    place = lax.broadcasted_iota(jnp.int32, (extra, LANES), 0)
    tail = jnp.where(place == 0, high.astype(F32), jnp.where(place == 1, low.astype(F32), 0.0))
    for at in range(out_ref.shape[0]):
        shard = [
            flat[at * rows : (at + 1) * rows, part * LANES : (part + 1) * LANES]
            for part in range(PARTS)
        ]
        out_ref[at] = jnp.concatenate(shard + [tail], axis=0).astype(BF16)


def gradients(block_at, key_rows, value_rows, step_rates, weights, shards, rows, padded):
    _, tokens, width = key_rows.shape
    heads = width // DH
    first = len(weights) == 3
    matrix = pl.BlockSpec((None, DH, DH), lambda h: (h, 0, 0))
    per_head = shards // heads
    packed = pl.BlockSpec((per_head, padded, LANES), lambda h: (h, 0, 0))
    rowed = pl.BlockSpec((None, tokens, DH), lambda h: (block_at, 0, h))
    return pl.pallas_call(
        functools.partial(gradient_kernel, first, block_at, rows),
        grid=(heads,),
        in_specs=[rowed, rowed, pl.BlockSpec((None, step_rates.shape[1], tokens), lambda h: (h, 0, 0))]
        + ([matrix] * 3 if first else [packed]),
        out_specs=packed,
        out_shape=pltpu.HBM((shards, padded, LANES), BF16),
        compiler_params=None if first else MID,
        scratch_shapes=[pltpu.VMEM((3 * DH, DH), F32)],
        cost_estimate=cost(heads * 12 * tokens * DH * DH, 8e6, heads * tokens * DH * 2),
        name="gradients",
    )(in_hbm(key_rows), in_hbm(value_rows), in_hbm(step_rates), *weights)


def row_scale(matrix):
    return jnp.sqrt(jnp.mean(matrix * matrix, axis=-1, keepdims=True) + EPSILON)


def shard_scale(shard, rows):
    square = jnp.sum(shard * shard, axis=-1, keepdims=True)
    total = sum(square[part * rows : (part + 1) * rows] for part in range(PARTS))
    return jnp.sqrt(total / DH + EPSILON)


def update_kernel(rows, parts_ref, old_ref, new_ref, copies_ref):
    total = parts_ref[0].astype(F32)
    for at in range(1, parts_ref.shape[0]):
        total += parts_ref[at].astype(F32)
    top = PARTS * rows
    rate = total[top : top + 1, :] + total[top + 1 : top + 2, :]
    old = old_ref[...]
    updated = old + total / rate
    ratio = shard_scale(old, rows) / shard_scale(updated, rows)
    rest = jnp.ones((old.shape[0] - top, 1), F32)
    new = updated * jnp.concatenate([ratio] * PARTS + [rest], axis=0)
    new_ref[...] = new
    rounded = new.astype(BF16)
    for at in range(copies_ref.shape[0]):
        copies_ref[at] = rounded


def update(parts, old, rows):
    shards, padded, _ = parts.shape
    return pl.pallas_call(
        functools.partial(update_kernel, rows),
        out_shape=(
            jax.ShapeDtypeStruct((padded, LANES), F32),
            jax.ShapeDtypeStruct((shards, padded, LANES), BF16),
        ),
        in_specs=[pl.BlockSpec(memory_space=pltpu.VMEM)] * 2,
        out_specs=(pl.BlockSpec(memory_space=pltpu.VMEM),) * 2,
        compiler_params=LEAN,
        cost_estimate=cost(2 * shards * padded * LANES, 4e6),
        name="update",
    )(parts, old)


def attend(query_ref, keys, values, out_ref, barred):
    scale = 1.0 / math.sqrt(DH)
    span = WINDOW + QUERY_TILE
    row = lax.broadcasted_iota(jnp.int32, (QUERY_TILE, span), 0)
    column = lax.broadcasted_iota(jnp.int32, (QUERY_TILE, span), 1)
    window = (column > row) & (column <= row + WINDOW)
    for at in range(query_ref.shape[0] // QUERY_TILE):
        low = at * QUERY_TILE
        scores = dot(query_ref[low : low + QUERY_TILE, :], keys[low : low + span, :], NT) * scale
        allowed = window if barred is None else window & (column + low >= barred)
        scores = jnp.where(allowed, scores, -jnp.inf)
        expos = jnp.exp(scores - jnp.max(scores, axis=1, keepdims=True))
        weights = (expos * (1.0 / jnp.sum(expos, axis=1, keepdims=True))).astype(BF16)
        mixed = dot(weights, values[low : low + span, :], NN)
        out_ref[low : low + QUERY_TILE, :] = mixed.astype(BF16)


def local_kernel(query_ref, key_ref, value_ref, out_ref):
    attend(query_ref, key_ref, value_ref, out_ref, None)


def attention_cost(blocks, heads):
    pairs = blocks * heads * WINDOW * (WINDOW + QUERY_TILE)
    return cost(4 * pairs * DH, 10e6, pairs)


def local_attention(queries, key_rows, value_rows):
    blocks, tokens, width = queries.shape
    heads = width // DH
    last = tokens // WINDOW - 1
    return pl.pallas_call(
        local_kernel,
        grid=(blocks, heads),
        in_specs=[
            pl.BlockSpec((None, WINDOW, DH), lambda b, h: (b, last, h)),
            pl.BlockSpec((None, tokens, DH), lambda b, h: (b, 0, h)),
            pl.BlockSpec((None, tokens, DH), lambda b, h: (b, 0, h)),
        ],
        out_specs=pl.BlockSpec((None, WINDOW, DH), lambda b, h: (b, 0, h)),
        out_shape=jax.ShapeDtypeStruct((blocks, WINDOW, width), BF16),
        cost_estimate=attention_cost(blocks, heads),
        name="local_attention",
    )(queries, key_rows, value_rows)


def near_kernel(block_at, place_ref, query_ref, key_ref, value_ref, *refs):
    near, (out_ref, keys, values) = refs[:-3], refs[-3:]
    keys[WINDOW:, :] = key_ref[...]
    values[WINDOW:, :] = value_ref[...]
    keys[:WINDOW, :] = near[0][...]
    values[:WINDOW, :] = near[1][...]
    first = place_ref[0] == 0
    barred = None
    if block_at == 0:
        barred = jnp.where(first, WINDOW, 0)
    else:

        @pl.when(first)
        def _():
            keys[:WINDOW, :] = near[2][...]
            values[:WINDOW, :] = near[3][...]

    attend(query_ref, keys, values, out_ref, barred)


def near_attention(block_at, place, queries, key_rows, value_rows, near):
    width = queries.shape[2]
    heads = width // DH
    own = pl.BlockSpec((None, WINDOW, DH), lambda h, place: (block_at, 0, h))
    rows = pl.BlockSpec((WINDOW, DH), lambda h, place: (0, h))
    return pl.pallas_call(
        functools.partial(near_kernel, block_at),
        grid_spec=pltpu.PrefetchScalarGridSpec(
            num_scalar_prefetch=1,
            grid=(heads,),
            in_specs=[own] * 3 + [rows] * len(near),
            out_specs=rows,
            scratch_shapes=[pltpu.VMEM((2 * WINDOW, DH), BF16)] * 2,
        ),
        out_shape=jax.ShapeDtypeStruct((WINDOW, width), BF16),
        cost_estimate=attention_cost(1, heads),
        name="near_attention",
    )(place, queries, key_rows, value_rows, *near)


def query_kernel(rows, query_ref, packed_ref, near_ref, local_ref, out_ref, flat):
    load_packed(packed_ref, flat, rows)
    gate, up = flat[:DH, :].astype(BF16), flat[DH : 2 * DH, :].astype(BF16)
    down = flat[2 * DH :, :].astype(BF16)
    for at in range(query_ref.shape[0] // WINDOW):
        piece = slice(at * WINDOW, (at + 1) * WINDOW)
        query = query_ref[piece, :]
        pre_gate = dot(query, gate, NT)
        hidden = (pre_gate * jax.nn.sigmoid(pre_gate) * dot(query, up, NT)).astype(BF16)
        fast = dot(hidden, down, NT)
        fast = fast / row_scale(fast)
        attended = (near_ref if at == 0 else local_ref)[...].astype(F32)
        out_ref[piece, :] = (fast + attended).astype(BF16)


def query_heads(block_at, queries, packed, near, local, rows, params, kept):
    _, tokens, width = queries.shape
    shards, padded, _ = packed.shape
    heads = width // DH
    per_head = shards // heads
    return pl.pallas_call(
        functools.partial(query_kernel, rows),
        grid=(heads,),
        in_specs=[
            pl.BlockSpec((None, tokens, DH), lambda h: (block_at, 0, h)),
            pl.BlockSpec((per_head, padded, LANES), lambda h: (h, 0, 0)),
            pl.BlockSpec((WINDOW, DH), lambda h: (0, h)),
            pl.BlockSpec((None, WINDOW, DH), lambda h: (block_at, 0, h)),
        ],
        out_specs=pl.BlockSpec((tokens, DH), lambda h: (0, h)),
        out_shape=kept((tokens, heads * DH), BF16),
        scratch_shapes=[pltpu.VMEM((3 * DH, DH), F32)],
        compiler_params=params,
        cost_estimate=cost(heads * 6 * tokens * DH * DH, heads * 3.5e6, heads * tokens * DH),
        name="query_heads",
    )(in_hbm(queries), packed, in_hbm(near), in_hbm(local))


def project_kernel(terms, has_sum, side_ref, *refs):
    out_ref = refs[-1]
    total = refs[2 * terms][...] if has_sum else None
    for at in range(terms):
        term = dot(refs[2 * at][...], refs[2 * at + 1][...], NN)
        total = term if total is None else total + term
    out_ref[...] = total.astype(out_ref.dtype)


def project(side, terms, tokens, summed=None, into=None, block_at=0, blocks=0, params=None):
    tile = 256
    specs, operands = [], []
    columns = terms[0][1].shape[0]
    for array, weight, first, own in terms:
        depth = array.shape[1]
        operands += [array, weight]
        specs.append(pl.BlockSpec((tile, depth), lambda t, side: (t, 0)))
        specs.append(
            pl.BlockSpec(
                (depth, columns),
                lambda t, side, first=first, own=own: (first, side[0] if own else 0),
            )
        )
    if summed is not None:
        operands.append(summed)
        specs.append(pl.BlockSpec((tile, columns), lambda t, side: (t, 0)))
    if into is not None:
        operands.append(into)
        specs.append(pl.BlockSpec(memory_space=pl.ANY))
    if blocks:
        out_spec = pl.BlockSpec((None, tile, columns), lambda t, side: (block_at, t, 0))
        out_shape = jax.ShapeDtypeStruct((blocks, tokens, columns), BF16)
    else:
        out_spec = pl.BlockSpec((tile, columns), lambda t, side: (t, 0))
        out_shape = jax.ShapeDtypeStruct((tokens, columns), F32)
    depth = sum(term[0].shape[1] for term in terms)
    return pl.pallas_call(
        functools.partial(project_kernel, len(terms), summed is not None),
        grid_spec=pltpu.PrefetchScalarGridSpec(
            num_scalar_prefetch=1, grid=(tokens // tile,), in_specs=specs, out_specs=out_spec
        ),
        out_shape=out_shape,
        input_output_aliases={} if into is None else {len(operands): 0},
        compiler_params=params,
        cost_estimate=cost(2 * tokens * columns * depth, 6e6),
        name="project",
    )(side, *operands)


def shards(queries, key_rows, value_rows, step_rates, gate_init, up_init, down_init, out_weight):
    blocks, tokens, width = queries.shape
    heads = width // DH
    count = lax.axis_size("tok")
    place = lax.axis_index("tok")
    side = lax.axis_index("head")
    ring = [(i, (i + 1) % count) for i in range(count)]
    swap = [(0, 1), (1, 0)]
    rows = heads * 3 * DH // count
    padded = -(-(PARTS * rows + 2) // 8) * 8

    weights = (gate_init, up_init, down_init)
    near = [lax.ppermute(key_rows[0, tokens - WINDOW :, :], "tok", ring)]
    parts = gradients(0, key_rows, value_rows, step_rates, weights, count, rows, padded)
    later_keys, later_values, parts = lax.optimization_barrier((key_rows, value_rows, parts))
    for at, array in enumerate((later_keys, later_values) * blocks):
        if at:
            near.append(lax.ppermute(array[at // 2, tokens - WINDOW :, :], "tok", ring))
    sent_weight = lax.dynamic_slice_in_dim(out_weight, (1 - side) * width, width, 1)
    other_weight = in_hbm(lax.ppermute(sent_weight, "head", swap))

    exchange = lambda x: lax.all_to_all(x, "tok", split_axis=0, concat_axis=0, tiled=True)
    flat = jnp.concatenate([gate_init, up_init, down_init], axis=1).reshape(heads * 3 * DH, DH)
    held = lax.dynamic_slice_in_dim(flat, place * rows, rows, 0)
    held = [held[:, part * LANES : (part + 1) * LANES] for part in range(PARTS)]
    held = jnp.concatenate(held + [jnp.zeros((padded - PARTS * rows, LANES), F32)], axis=0)

    local = local_attention(queries, key_rows, value_rows)
    nears = []
    for block_at in range(blocks):
        reach = near[2 * block_at : 2 * block_at + 2] + near[: 2 * block_at][-2:]
        nears.append(
            near_attention(block_at, place.reshape(1), queries, key_rows, value_rows, reach)
        )
    result = None
    side_ref = side.reshape(1)
    for block_at in range(blocks):
        last = block_at == blocks - 1
        parts = exchange(parts)
        held, copies = update(parts, held, rows)
        packed = exchange(copies)
        near_now = nears[block_at]
        if not last:
            parts = gradients(
                block_at + 1, key_rows, value_rows, step_rates, (packed,), count, rows, padded
            )
            own = query_heads(
                block_at, queries, packed, near_now, local, rows, None, jax.ShapeDtypeStruct
            )
            other = lax.ppermute(own, "head", swap)
            terms = [(own, out_weight, 0, True), (other, other_weight, 0, False)]
            result = project(side_ref, terms, tokens, None, result, block_at, blocks)
            continue
        own = query_heads(
            block_at, queries, packed, near_now, local, rows, MID, pltpu.VMEM
        )
        other = lax.ppermute(own, "head", swap)
        terms = [(own, out_weight, 0, True), (other, other_weight, 0, False)]
        result = project(side_ref, terms, tokens, None, result, block_at, blocks, LEAN)
    return result


def solution(mesh):
    in_specs = (
        P(None, "tok", "head"),
        P(None, "tok", "head"),
        P(None, "tok", "head"),
        P("head", None, "tok"),
        P("head", None, None),
        P("head", None, None),
        P("head", None, None),
        P("head", None),
    )
    out_specs = P(None, "tok", "head")
    return jax.shard_map(shards, mesh=mesh, in_specs=in_specs, out_specs=out_specs, check_vma=False)
```

```python
import functools
import math

import jax
import jax.numpy as jnp
from jax import lax
from jax.experimental import pallas as pl
from jax.experimental.pallas import tpu as pltpu
from jax.sharding import PartitionSpec as P


DH = 384
WINDOW = 384
EPSILON = 1e-06
BF16 = jnp.bfloat16
F32 = jnp.float32
LANES = 128
PARTS = DH // LANES
MID = pltpu.CompilerParams(vmem_limit_bytes=48 * 2**20)
LEAN = pltpu.CompilerParams(vmem_limit_bytes=36 * 2**20)
QUERY_TILE = 128

NT = (((1,), (1,)), ((), ()))
NN = (((1,), (0,)), ((), ()))


def dot(a, b, dims):
    return lax.dot_general(a, b, dims, preferred_element_type=F32)


def cost(flops, bytes_accessed, transcendentals=0):
    return pl.CostEstimate(
        flops=int(flops), bytes_accessed=int(bytes_accessed), transcendentals=int(transcendentals)
    )


def load_packed(packed_ref, flat, rows):
    for at in range(packed_ref.shape[0]):
        shard = packed_ref[at].astype(F32)
        for part in range(PARTS):
            columns = slice(part * LANES, (part + 1) * LANES)
            flat[at * rows : (at + 1) * rows, columns] = shard[part * rows : (part + 1) * rows, :]


def gradient_kernel(first, block_at, rows, *refs):
    if first:
        key_ref, value_ref, rate_ref, gate_ref, up_ref, down_ref, out_ref, flat = refs
        gate, up = gate_ref[...].astype(BF16), up_ref[...].astype(BF16)
        down_t = jnp.transpose(down_ref[...]).astype(BF16)
    else:
        key_ref, value_ref, rate_ref, packed_ref, out_ref, flat = refs
        load_packed(packed_ref, flat, rows)
        gate, up = flat[:DH, :].astype(BF16), flat[DH : 2 * DH, :].astype(BF16)
        down_t = jnp.transpose(flat[2 * DH :, :]).astype(BF16)
    key, value = key_ref[...], value_ref[...]
    rate = rate_ref[block_at : block_at + 1, :]
    pre_gate = dot(gate, key, NT)
    pre_up = dot(up, key, NT)
    backed = dot(down_t, value, NT) * rate
    sigmoid = jax.nn.sigmoid(pre_gate)
    active = pre_gate * sigmoid
    hidden = (active * pre_up * rate).astype(BF16)
    to_up = (backed * active).astype(BF16)
    slope = sigmoid * (1.0 + pre_gate * (1.0 - sigmoid))
    to_gate = (backed * pre_up * slope).astype(BF16)
    flat[:DH, :] = dot(to_gate, key, NN)
    flat[DH : 2 * DH, :] = dot(to_up, key, NN)
    flat[2 * DH :, :] = jnp.transpose(dot(hidden, value, NN))
    total = jnp.sum(rate, axis=1, keepdims=True)
    high = total.astype(BF16)
    low = (total - high.astype(F32)).astype(BF16)
    extra = out_ref.shape[1] - PARTS * rows
    place = lax.broadcasted_iota(jnp.int32, (extra, LANES), 0)
    tail = jnp.where(place == 0, high.astype(F32), jnp.where(place == 1, low.astype(F32), 0.0))
    for at in range(out_ref.shape[0]):
        shard = [
            flat[at * rows : (at + 1) * rows, part * LANES : (part + 1) * LANES]
            for part in range(PARTS)
        ]
        out_ref[at] = jnp.concatenate(shard + [tail], axis=0).astype(BF16)


def gradients(block_at, key_rows, value_rows, step_rates, weights, shards, rows, padded):
    _, tokens, width = key_rows.shape
    heads = width // DH
    first = len(weights) == 3
    matrix = pl.BlockSpec((None, DH, DH), lambda h: (h, 0, 0))
    per_head = shards // heads
    packed = pl.BlockSpec((per_head, padded, LANES), lambda h: (h, 0, 0))
    rowed = pl.BlockSpec((None, tokens, DH), lambda h: (block_at, 0, h))
    return pl.pallas_call(
        functools.partial(gradient_kernel, first, block_at, rows),
        grid=(heads,),
        in_specs=[rowed, rowed, pl.BlockSpec((None, step_rates.shape[1], tokens), lambda h: (h, 0, 0))]
        + ([matrix] * 3 if first else [packed]),
        out_specs=packed,
        out_shape=jax.ShapeDtypeStruct((shards, padded, LANES), BF16),
        scratch_shapes=[pltpu.VMEM((3 * DH, DH), F32)],
        cost_estimate=cost(heads * 12 * tokens * DH * DH, 8e6, heads * tokens * DH * 2),
        name="gradients",
    )(key_rows, value_rows, step_rates, *weights)


def row_scale(matrix):
    return jnp.sqrt(jnp.mean(matrix * matrix, axis=-1, keepdims=True) + EPSILON)


def shard_scale(shard, rows):
    square = jnp.sum(shard * shard, axis=-1, keepdims=True)
    total = sum(square[part * rows : (part + 1) * rows] for part in range(PARTS))
    return jnp.sqrt(total / DH + EPSILON)


def update_kernel(rows, parts_ref, old_ref, new_ref, copies_ref):
    total = parts_ref[0].astype(F32)
    for at in range(1, parts_ref.shape[0]):
        total += parts_ref[at].astype(F32)
    top = PARTS * rows
    rate = total[top : top + 1, :] + total[top + 1 : top + 2, :]
    old = old_ref[...]
    updated = old + total / rate
    ratio = shard_scale(old, rows) / shard_scale(updated, rows)
    rest = jnp.ones((old.shape[0] - top, 1), F32)
    new = updated * jnp.concatenate([ratio] * PARTS + [rest], axis=0)
    new_ref[...] = new
    rounded = new.astype(BF16)
    for at in range(copies_ref.shape[0]):
        copies_ref[at] = rounded


def update(parts, old, rows):
    shards, padded, _ = parts.shape
    return pl.pallas_call(
        functools.partial(update_kernel, rows),
        out_shape=(
            jax.ShapeDtypeStruct((padded, LANES), F32),
            jax.ShapeDtypeStruct((shards, padded, LANES), BF16),
        ),
        in_specs=[pl.BlockSpec(memory_space=pltpu.VMEM)] * 2,
        out_specs=(pl.BlockSpec(memory_space=pltpu.VMEM),) * 2,
        compiler_params=LEAN,
        cost_estimate=cost(2 * shards * padded * LANES, 4e6),
        name="update",
    )(parts, old)


def attend(query_ref, keys, values, out_ref, barred):
    scale = 1.0 / math.sqrt(DH)
    span = WINDOW + QUERY_TILE
    row = lax.broadcasted_iota(jnp.int32, (QUERY_TILE, span), 0)
    column = lax.broadcasted_iota(jnp.int32, (QUERY_TILE, span), 1)
    window = (column > row) & (column <= row + WINDOW)
    for at in range(query_ref.shape[0] // QUERY_TILE):
        low = at * QUERY_TILE
        scores = dot(query_ref[low : low + QUERY_TILE, :], keys[low : low + span, :], NT) * scale
        allowed = window if barred is None else window & (column + low >= barred)
        scores = jnp.where(allowed, scores, -jnp.inf)
        expos = jnp.exp(scores - jnp.max(scores, axis=1, keepdims=True))
        weights = (expos * (1.0 / jnp.sum(expos, axis=1, keepdims=True))).astype(BF16)
        mixed = dot(weights, values[low : low + span, :], NN)
        out_ref[low : low + QUERY_TILE, :] = mixed.astype(BF16)


def local_kernel(query_ref, key_ref, value_ref, out_ref):
    attend(query_ref, key_ref, value_ref, out_ref, None)


def attention_cost(blocks, heads):
    pairs = blocks * heads * WINDOW * (WINDOW + QUERY_TILE)
    return cost(4 * pairs * DH, 10e6, pairs)


def local_attention(queries, key_rows, value_rows):
    blocks, tokens, width = queries.shape
    heads = width // DH
    last = tokens // WINDOW - 1
    return pl.pallas_call(
        local_kernel,
        grid=(blocks, heads),
        in_specs=[
            pl.BlockSpec((None, WINDOW, DH), lambda b, h: (b, last, h)),
            pl.BlockSpec((None, tokens, DH), lambda b, h: (b, 0, h)),
            pl.BlockSpec((None, tokens, DH), lambda b, h: (b, 0, h)),
        ],
        out_specs=pl.BlockSpec((None, WINDOW, DH), lambda b, h: (b, 0, h)),
        out_shape=jax.ShapeDtypeStruct((blocks, WINDOW, width), BF16),
        cost_estimate=attention_cost(blocks, heads),
        name="local_attention",
    )(queries, key_rows, value_rows)


def near_kernel(block_at, place_ref, query_ref, key_ref, value_ref, *refs):
    near, (out_ref, keys, values) = refs[:-3], refs[-3:]
    keys[WINDOW:, :] = key_ref[...]
    values[WINDOW:, :] = value_ref[...]
    keys[:WINDOW, :] = near[0][...]
    values[:WINDOW, :] = near[1][...]
    first = place_ref[0] == 0
    barred = None
    if block_at == 0:
        barred = jnp.where(first, WINDOW, 0)
    else:

        @pl.when(first)
        def _():
            keys[:WINDOW, :] = near[2][...]
            values[:WINDOW, :] = near[3][...]

    attend(query_ref, keys, values, out_ref, barred)


def near_attention(block_at, place, queries, key_rows, value_rows, near):
    width = queries.shape[2]
    heads = width // DH
    own = pl.BlockSpec((None, WINDOW, DH), lambda h, place: (block_at, 0, h))
    rows = pl.BlockSpec((WINDOW, DH), lambda h, place: (0, h))
    return pl.pallas_call(
        functools.partial(near_kernel, block_at),
        grid_spec=pltpu.PrefetchScalarGridSpec(
            num_scalar_prefetch=1,
            grid=(heads,),
            in_specs=[own] * 3 + [rows] * len(near),
            out_specs=rows,
            scratch_shapes=[pltpu.VMEM((2 * WINDOW, DH), BF16)] * 2,
        ),
        out_shape=jax.ShapeDtypeStruct((WINDOW, width), BF16),
        cost_estimate=attention_cost(1, heads),
        name="near_attention",
    )(place, queries, key_rows, value_rows, *near)


def query_kernel(rows, query_ref, packed_ref, near_ref, local_ref, out_ref, flat):
    load_packed(packed_ref, flat, rows)
    gate, up = flat[:DH, :].astype(BF16), flat[DH : 2 * DH, :].astype(BF16)
    down = flat[2 * DH :, :].astype(BF16)
    for at in range(query_ref.shape[0] // WINDOW):
        piece = slice(at * WINDOW, (at + 1) * WINDOW)
        query = query_ref[piece, :]
        pre_gate = dot(query, gate, NT)
        hidden = (pre_gate * jax.nn.sigmoid(pre_gate) * dot(query, up, NT)).astype(BF16)
        fast = dot(hidden, down, NT)
        fast = fast / row_scale(fast)
        attended = (near_ref if at == 0 else local_ref)[...].astype(F32)
        out_ref[piece, :] = (fast + attended).astype(BF16)


def in_hbm(array):
    return pltpu.with_memory_space_constraint(array, pltpu.HBM)


def query_heads(block_at, queries, packed, near, local, rows, params, kept):
    _, tokens, width = queries.shape
    shards, padded, _ = packed.shape
    heads = width // DH
    per_head = shards // heads
    return pl.pallas_call(
        functools.partial(query_kernel, rows),
        grid=(heads,),
        in_specs=[
            pl.BlockSpec((None, tokens, DH), lambda h: (block_at, 0, h)),
            pl.BlockSpec((per_head, padded, LANES), lambda h: (h, 0, 0)),
            pl.BlockSpec((WINDOW, DH), lambda h: (0, h)),
            pl.BlockSpec((None, WINDOW, DH), lambda h: (block_at, 0, h)),
        ],
        out_specs=pl.BlockSpec((tokens, DH), lambda h: (0, h)),
        out_shape=kept((tokens, heads * DH), BF16),
        scratch_shapes=[pltpu.VMEM((3 * DH, DH), F32)],
        compiler_params=params,
        cost_estimate=cost(heads * 6 * tokens * DH * DH, heads * 3.5e6, heads * tokens * DH),
        name="query_heads",
    )(queries, packed, in_hbm(near), in_hbm(local))


def project_kernel(terms, has_sum, side_ref, *refs):
    out_ref = refs[-1]
    total = refs[2 * terms][...] if has_sum else None
    for at in range(terms):
        term = dot(refs[2 * at][...], refs[2 * at + 1][...], NN)
        total = term if total is None else total + term
    out_ref[...] = total.astype(out_ref.dtype)


def project(side, terms, tokens, summed=None, into=None, block_at=0, blocks=0, params=None):
    tile = 256
    specs, operands = [], []
    columns = terms[0][1].shape[0]
    for array, weight, first, own in terms:
        depth = array.shape[1]
        operands += [array, weight]
        specs.append(pl.BlockSpec((tile, depth), lambda t, side: (t, 0)))
        specs.append(
            pl.BlockSpec(
                (depth, columns),
                lambda t, side, first=first, own=own: (first, side[0] if own else 0),
            )
        )
    if summed is not None:
        operands.append(summed)
        specs.append(pl.BlockSpec((tile, columns), lambda t, side: (t, 0)))
    if into is not None:
        operands.append(into)
        specs.append(pl.BlockSpec(memory_space=pl.ANY))
    if blocks:
        out_spec = pl.BlockSpec((None, tile, columns), lambda t, side: (block_at, t, 0))
        out_shape = jax.ShapeDtypeStruct((blocks, tokens, columns), BF16)
    else:
        out_spec = pl.BlockSpec((tile, columns), lambda t, side: (t, 0))
        out_shape = jax.ShapeDtypeStruct((tokens, columns), F32)
    depth = sum(term[0].shape[1] for term in terms)
    return pl.pallas_call(
        functools.partial(project_kernel, len(terms), summed is not None),
        grid_spec=pltpu.PrefetchScalarGridSpec(
            num_scalar_prefetch=1, grid=(tokens // tile,), in_specs=specs, out_specs=out_spec
        ),
        out_shape=out_shape,
        input_output_aliases={} if into is None else {len(operands): 0},
        compiler_params=params,
        cost_estimate=cost(2 * tokens * columns * depth, 6e6),
        name="project",
    )(side, *operands)


def shards(queries, key_rows, value_rows, step_rates, gate_init, up_init, down_init, out_weight):
    blocks, tokens, width = queries.shape
    heads = width // DH
    count = lax.axis_size("tok")
    place = lax.axis_index("tok")
    side = lax.axis_index("head")
    ring = [(i, (i + 1) % count) for i in range(count)]
    swap = [(0, 1), (1, 0)]
    rows = heads * 3 * DH // count
    padded = -(-(PARTS * rows + 2) // 8) * 8

    weights = (gate_init, up_init, down_init)
    near = [lax.ppermute(key_rows[0, tokens - WINDOW :, :], "tok", ring)]
    parts = gradients(0, key_rows, value_rows, step_rates, weights, count, rows, padded)
    later_keys, later_values, parts = lax.optimization_barrier((key_rows, value_rows, parts))
    for at, array in enumerate((later_keys, later_values) * blocks):
        if at:
            near.append(lax.ppermute(array[at // 2, tokens - WINDOW :, :], "tok", ring))
    sent_weight = lax.dynamic_slice_in_dim(out_weight, (1 - side) * width, width, 1)
    other_weight = lax.ppermute(sent_weight, "head", swap)

    exchange = lambda x: lax.all_to_all(x, "tok", split_axis=0, concat_axis=0, tiled=True)
    flat = jnp.concatenate([gate_init, up_init, down_init], axis=1).reshape(heads * 3 * DH, DH)
    held = lax.dynamic_slice_in_dim(flat, place * rows, rows, 0)
    held = [held[:, part * LANES : (part + 1) * LANES] for part in range(PARTS)]
    held = jnp.concatenate(held + [jnp.zeros((padded - PARTS * rows, LANES), F32)], axis=0)

    local = local_attention(queries, key_rows, value_rows)
    nears = []
    for block_at in range(blocks):
        reach = near[2 * block_at : 2 * block_at + 2] + near[: 2 * block_at][-2:]
        nears.append(
            near_attention(block_at, place.reshape(1), queries, key_rows, value_rows, reach)
        )
    result = None
    side_ref = side.reshape(1)
    for block_at in range(blocks):
        last = block_at == blocks - 1
        parts = exchange(parts)
        held, copies = update(parts, held, rows)
        packed = exchange(copies)
        near_now = nears[block_at]
        if not last:
            parts = gradients(
                block_at + 1, key_rows, value_rows, step_rates, (packed,), count, rows, padded
            )
            own = query_heads(
                block_at, queries, packed, near_now, local, rows, None, jax.ShapeDtypeStruct
            )
            other = lax.ppermute(own, "head", swap)
            terms = [(own, out_weight, 0, True), (other, other_weight, 0, False)]
            result = project(side_ref, terms, tokens, None, result, block_at, blocks)
            continue
        own = query_heads(
            block_at, queries, packed, near_now, local, rows, MID, pltpu.VMEM
        )
        other = lax.ppermute(own, "head", swap)
        terms = [(own, out_weight, 0, True), (other, other_weight, 0, False)]
        result = project(side_ref, terms, tokens, None, result, block_at, blocks, LEAN)
    return result


def solution(mesh):
    in_specs = (
        P(None, "tok", "head"),
        P(None, "tok", "head"),
        P(None, "tok", "head"),
        P("head", None, "tok"),
        P("head", None, None),
        P("head", None, None),
        P("head", None, None),
        P("head", None),
    )
    out_specs = P(None, "tok", "head")
    return jax.shard_map(shards, mesh=mesh, in_specs=in_specs, out_specs=out_specs, check_vma=False)
```

```python
import functools
import math

import jax
import jax.numpy as jnp
from jax import lax
from jax.experimental import pallas as pl
from jax.experimental.pallas import tpu as pltpu
from jax.sharding import PartitionSpec as P


DH = 384
WINDOW = 384
EPSILON = 1e-06
BF16 = jnp.bfloat16
F32 = jnp.float32
LANES = 128
PARTS = DH // LANES
MID = pltpu.CompilerParams(vmem_limit_bytes=48 * 2**20)
LEAN = pltpu.CompilerParams(vmem_limit_bytes=36 * 2**20)
QUERY_TILE = 128

NT = (((1,), (1,)), ((), ()))
NN = (((1,), (0,)), ((), ()))


def dot(a, b, dims):
    return lax.dot_general(a, b, dims, preferred_element_type=F32)


def cost(flops, bytes_accessed, transcendentals=0):
    return pl.CostEstimate(
        flops=int(flops), bytes_accessed=int(bytes_accessed), transcendentals=int(transcendentals)
    )


def load_packed(packed_ref, flat, rows):
    for at in range(packed_ref.shape[0]):
        shard = packed_ref[at].astype(F32)
        for part in range(PARTS):
            columns = slice(part * LANES, (part + 1) * LANES)
            flat[at * rows : (at + 1) * rows, columns] = shard[part * rows : (part + 1) * rows, :]


def gradient_kernel(first, block_at, rows, *refs):
    if first:
        key_ref, value_ref, rate_ref, gate_ref, up_ref, down_ref, out_ref, flat = refs
        gate, up = gate_ref[...].astype(BF16), up_ref[...].astype(BF16)
        down_t = jnp.transpose(down_ref[...]).astype(BF16)
    else:
        key_ref, value_ref, rate_ref, packed_ref, out_ref, flat = refs
        load_packed(packed_ref, flat, rows)
        gate, up = flat[:DH, :].astype(BF16), flat[DH : 2 * DH, :].astype(BF16)
        down_t = jnp.transpose(flat[2 * DH :, :]).astype(BF16)
    key, value = key_ref[...], value_ref[...]
    rate = rate_ref[block_at : block_at + 1, :]
    pre_gate = dot(gate, key, NT)
    pre_up = dot(up, key, NT)
    backed = dot(down_t, value, NT) * rate
    sigmoid = jax.nn.sigmoid(pre_gate)
    active = pre_gate * sigmoid
    hidden = (active * pre_up * rate).astype(BF16)
    to_up = (backed * active).astype(BF16)
    slope = sigmoid * (1.0 + pre_gate * (1.0 - sigmoid))
    to_gate = (backed * pre_up * slope).astype(BF16)
    flat[:DH, :] = dot(to_gate, key, NN)
    flat[DH : 2 * DH, :] = dot(to_up, key, NN)
    flat[2 * DH :, :] = jnp.transpose(dot(hidden, value, NN))
    total = jnp.sum(rate, axis=1, keepdims=True)
    high = total.astype(BF16)
    low = (total - high.astype(F32)).astype(BF16)
    extra = out_ref.shape[1] - PARTS * rows
    place = lax.broadcasted_iota(jnp.int32, (extra, LANES), 0)
    tail = jnp.where(place == 0, high.astype(F32), jnp.where(place == 1, low.astype(F32), 0.0))
    for at in range(out_ref.shape[0]):
        shard = [
            flat[at * rows : (at + 1) * rows, part * LANES : (part + 1) * LANES]
            for part in range(PARTS)
        ]
        out_ref[at] = jnp.concatenate(shard + [tail], axis=0).astype(BF16)


def gradients(block_at, key_rows, value_rows, step_rates, weights, shards, rows, padded):
    _, tokens, width = key_rows.shape
    heads = width // DH
    first = len(weights) == 3
    matrix = pl.BlockSpec((None, DH, DH), lambda h: (h, 0, 0))
    per_head = shards // heads
    packed = pl.BlockSpec((per_head, padded, LANES), lambda h: (h, 0, 0))
    rowed = pl.BlockSpec((None, tokens, DH), lambda h: (block_at, 0, h))
    return pl.pallas_call(
        functools.partial(gradient_kernel, first, block_at, rows),
        grid=(heads,),
        in_specs=[rowed, rowed, pl.BlockSpec((None, step_rates.shape[1], tokens), lambda h: (h, 0, 0))]
        + ([matrix] * 3 if first else [packed]),
        out_specs=packed,
        out_shape=jax.ShapeDtypeStruct((shards, padded, LANES), BF16),
        scratch_shapes=[pltpu.VMEM((3 * DH, DH), F32)],
        cost_estimate=cost(heads * 12 * tokens * DH * DH, 8e6, heads * tokens * DH * 2),
        name="gradients",
    )(key_rows, value_rows, step_rates, *weights)


def row_scale(matrix):
    return jnp.sqrt(jnp.mean(matrix * matrix, axis=-1, keepdims=True) + EPSILON)


def shard_scale(shard, rows):
    square = jnp.sum(shard * shard, axis=-1, keepdims=True)
    total = sum(square[part * rows : (part + 1) * rows] for part in range(PARTS))
    return jnp.sqrt(total / DH + EPSILON)


def update_kernel(rows, parts_ref, old_ref, new_ref, copies_ref):
    total = parts_ref[0].astype(F32)
    for at in range(1, parts_ref.shape[0]):
        total += parts_ref[at].astype(F32)
    top = PARTS * rows
    rate = total[top : top + 1, :] + total[top + 1 : top + 2, :]
    old = old_ref[...]
    updated = old + total / rate
    ratio = shard_scale(old, rows) / shard_scale(updated, rows)
    rest = jnp.ones((old.shape[0] - top, 1), F32)
    new = updated * jnp.concatenate([ratio] * PARTS + [rest], axis=0)
    new_ref[...] = new
    rounded = new.astype(BF16)
    for at in range(copies_ref.shape[0]):
        copies_ref[at] = rounded


def update(parts, old, rows):
    shards, padded, _ = parts.shape
    return pl.pallas_call(
        functools.partial(update_kernel, rows),
        out_shape=(
            jax.ShapeDtypeStruct((padded, LANES), F32),
            jax.ShapeDtypeStruct((shards, padded, LANES), BF16),
        ),
        in_specs=[pl.BlockSpec(memory_space=pltpu.VMEM)] * 2,
        out_specs=(pl.BlockSpec(memory_space=pltpu.VMEM),) * 2,
        compiler_params=LEAN,
        cost_estimate=cost(2 * shards * padded * LANES, 4e6),
        name="update",
    )(parts, old)


def attend(query_ref, keys, values, out_ref, barred):
    scale = 1.0 / math.sqrt(DH)
    span = WINDOW + QUERY_TILE
    row = lax.broadcasted_iota(jnp.int32, (QUERY_TILE, span), 0)
    column = lax.broadcasted_iota(jnp.int32, (QUERY_TILE, span), 1)
    window = (column > row) & (column <= row + WINDOW)
    for at in range(query_ref.shape[0] // QUERY_TILE):
        low = at * QUERY_TILE
        scores = dot(query_ref[low : low + QUERY_TILE, :], keys[low : low + span, :], NT) * scale
        allowed = window if barred is None else window & (column + low >= barred)
        scores = jnp.where(allowed, scores, -jnp.inf)
        expos = jnp.exp(scores - jnp.max(scores, axis=1, keepdims=True))
        weights = (expos * (1.0 / jnp.sum(expos, axis=1, keepdims=True))).astype(BF16)
        mixed = dot(weights, values[low : low + span, :], NN)
        out_ref[low : low + QUERY_TILE, :] = mixed.astype(BF16)


def local_kernel(query_ref, key_ref, value_ref, out_ref):
    attend(query_ref, key_ref, value_ref, out_ref, None)


def attention_cost(blocks, heads):
    pairs = blocks * heads * WINDOW * (WINDOW + QUERY_TILE)
    return cost(4 * pairs * DH, 10e6, pairs)


def local_attention(queries, key_rows, value_rows):
    blocks, tokens, width = queries.shape
    heads = width // DH
    last = tokens // WINDOW - 1
    return pl.pallas_call(
        local_kernel,
        grid=(blocks, heads),
        in_specs=[
            pl.BlockSpec((None, WINDOW, DH), lambda b, h: (b, last, h)),
            pl.BlockSpec((None, tokens, DH), lambda b, h: (b, 0, h)),
            pl.BlockSpec((None, tokens, DH), lambda b, h: (b, 0, h)),
        ],
        out_specs=pl.BlockSpec((None, WINDOW, DH), lambda b, h: (b, 0, h)),
        out_shape=jax.ShapeDtypeStruct((blocks, WINDOW, width), BF16),
        cost_estimate=attention_cost(blocks, heads),
        name="local_attention",
    )(queries, key_rows, value_rows)


def near_kernel(block_at, place_ref, query_ref, key_ref, value_ref, *refs):
    near, (out_ref, keys, values) = refs[:-3], refs[-3:]
    keys[WINDOW:, :] = key_ref[...]
    values[WINDOW:, :] = value_ref[...]
    keys[:WINDOW, :] = near[0][...]
    values[:WINDOW, :] = near[1][...]
    first = place_ref[0] == 0
    barred = None
    if block_at == 0:
        barred = jnp.where(first, WINDOW, 0)
    else:

        @pl.when(first)
        def _():
            keys[:WINDOW, :] = near[2][...]
            values[:WINDOW, :] = near[3][...]

    attend(query_ref, keys, values, out_ref, barred)


def near_attention(block_at, place, queries, key_rows, value_rows, near):
    width = queries.shape[2]
    heads = width // DH
    own = pl.BlockSpec((None, WINDOW, DH), lambda h, place: (block_at, 0, h))
    rows = pl.BlockSpec((WINDOW, DH), lambda h, place: (0, h))
    return pl.pallas_call(
        functools.partial(near_kernel, block_at),
        grid_spec=pltpu.PrefetchScalarGridSpec(
            num_scalar_prefetch=1,
            grid=(heads,),
            in_specs=[own] * 3 + [rows] * len(near),
            out_specs=rows,
            scratch_shapes=[pltpu.VMEM((2 * WINDOW, DH), BF16)] * 2,
        ),
        out_shape=jax.ShapeDtypeStruct((WINDOW, width), BF16),
        cost_estimate=attention_cost(1, heads),
        name="near_attention",
    )(place, queries, key_rows, value_rows, *near)


def query_kernel(rows, query_ref, packed_ref, near_ref, local_ref, out_ref, flat):
    load_packed(packed_ref, flat, rows)
    gate, up = flat[:DH, :].astype(BF16), flat[DH : 2 * DH, :].astype(BF16)
    down = flat[2 * DH :, :].astype(BF16)
    query = query_ref[...]
    pre_gate = dot(query, gate, NT)
    hidden = (pre_gate * jax.nn.sigmoid(pre_gate) * dot(query, up, NT)).astype(BF16)
    fast = dot(hidden, down, NT)
    fast = fast / row_scale(fast)
    out_ref[:WINDOW, :] = (fast[:WINDOW, :] + near_ref[...].astype(F32)).astype(BF16)
    out_ref[WINDOW:, :] = (fast[WINDOW:, :] + local_ref[...].astype(F32)).astype(BF16)


def in_hbm(array):
    return pltpu.with_memory_space_constraint(array, pltpu.HBM)


def query_heads(block_at, queries, packed, near, local, rows, params, kept):
    _, tokens, width = queries.shape
    shards, padded, _ = packed.shape
    heads = width // DH
    per_head = shards // heads
    return pl.pallas_call(
        functools.partial(query_kernel, rows),
        grid=(heads,),
        in_specs=[
            pl.BlockSpec((None, tokens, DH), lambda h: (block_at, 0, h)),
            pl.BlockSpec((per_head, padded, LANES), lambda h: (h, 0, 0)),
            pl.BlockSpec((WINDOW, DH), lambda h: (0, h)),
            pl.BlockSpec((None, WINDOW, DH), lambda h: (block_at, 0, h)),
        ],
        out_specs=pl.BlockSpec((tokens, DH), lambda h: (0, h)),
        out_shape=kept((tokens, heads * DH), BF16),
        scratch_shapes=[pltpu.VMEM((3 * DH, DH), F32)],
        compiler_params=params,
        cost_estimate=cost(heads * 6 * tokens * DH * DH, heads * 3.5e6, heads * tokens * DH),
        name="query_heads",
    )(in_hbm(queries), packed, in_hbm(near), in_hbm(local))


def project_kernel(terms, has_sum, side_ref, *refs):
    out_ref = refs[-1]
    total = refs[2 * terms][...] if has_sum else None
    for at in range(terms):
        term = dot(refs[2 * at][...], refs[2 * at + 1][...], NN)
        total = term if total is None else total + term
    out_ref[...] = total.astype(out_ref.dtype)


def project(side, terms, tokens, summed=None, into=None, block_at=0, blocks=0, params=None):
    tile = 256
    specs, operands = [], []
    columns = terms[0][1].shape[0]
    for array, weight, first, own in terms:
        depth = array.shape[1]
        operands += [array, weight]
        specs.append(pl.BlockSpec((tile, depth), lambda t, side: (t, 0)))
        specs.append(
            pl.BlockSpec(
                (depth, columns),
                lambda t, side, first=first, own=own: (first, side[0] if own else 0),
            )
        )
    if summed is not None:
        operands.append(summed)
        specs.append(pl.BlockSpec((tile, columns), lambda t, side: (t, 0)))
    if into is not None:
        operands.append(into)
        specs.append(pl.BlockSpec(memory_space=pl.ANY))
    if blocks:
        out_spec = pl.BlockSpec((None, tile, columns), lambda t, side: (block_at, t, 0))
        out_shape = jax.ShapeDtypeStruct((blocks, tokens, columns), BF16)
    else:
        out_spec = pl.BlockSpec((tile, columns), lambda t, side: (t, 0))
        out_shape = jax.ShapeDtypeStruct((tokens, columns), F32)
    depth = sum(term[0].shape[1] for term in terms)
    return pl.pallas_call(
        functools.partial(project_kernel, len(terms), summed is not None),
        grid_spec=pltpu.PrefetchScalarGridSpec(
            num_scalar_prefetch=1, grid=(tokens // tile,), in_specs=specs, out_specs=out_spec
        ),
        out_shape=out_shape,
        input_output_aliases={} if into is None else {len(operands): 0},
        compiler_params=params,
        cost_estimate=cost(2 * tokens * columns * depth, 6e6),
        name="project",
    )(side, *operands)


def shards(queries, key_rows, value_rows, step_rates, gate_init, up_init, down_init, out_weight):
    blocks, tokens, width = queries.shape
    heads = width // DH
    count = lax.axis_size("tok")
    place = lax.axis_index("tok")
    side = lax.axis_index("head")
    ring = [(i, (i + 1) % count) for i in range(count)]
    swap = [(0, 1), (1, 0)]
    rows = heads * 3 * DH // count
    padded = -(-(PARTS * rows + 2) // 8) * 8

    weights = (gate_init, up_init, down_init)
    near = [lax.ppermute(key_rows[0, tokens - WINDOW :, :], "tok", ring)]
    parts = gradients(0, key_rows, value_rows, step_rates, weights, count, rows, padded)
    later_keys, later_values, parts = lax.optimization_barrier((key_rows, value_rows, parts))
    for at, array in enumerate((later_keys, later_values) * blocks):
        if at:
            near.append(lax.ppermute(array[at // 2, tokens - WINDOW :, :], "tok", ring))
    sent_weight = lax.dynamic_slice_in_dim(out_weight, (1 - side) * width, width, 1)
    other_weight = lax.ppermute(sent_weight, "head", swap)

    exchange = lambda x: lax.all_to_all(x, "tok", split_axis=0, concat_axis=0, tiled=True)
    flat = jnp.concatenate([gate_init, up_init, down_init], axis=1).reshape(heads * 3 * DH, DH)
    held = lax.dynamic_slice_in_dim(flat, place * rows, rows, 0)
    held = [held[:, part * LANES : (part + 1) * LANES] for part in range(PARTS)]
    held = jnp.concatenate(held + [jnp.zeros((padded - PARTS * rows, LANES), F32)], axis=0)

    local = local_attention(queries, key_rows, value_rows)
    nears = []
    for block_at in range(blocks):
        reach = near[2 * block_at : 2 * block_at + 2] + near[: 2 * block_at][-2:]
        nears.append(
            near_attention(block_at, place.reshape(1), queries, key_rows, value_rows, reach)
        )
    result = None
    side_ref = side.reshape(1)
    for block_at in range(blocks):
        last = block_at == blocks - 1
        parts = exchange(parts)
        held, copies = update(parts, held, rows)
        packed = exchange(copies)
        near_now = nears[block_at]
        if not last:
            parts = gradients(
                block_at + 1, key_rows, value_rows, step_rates, (packed,), count, rows, padded
            )
            own = query_heads(
                block_at, queries, packed, near_now, local, rows, None, jax.ShapeDtypeStruct
            )
            other = lax.ppermute(own, "head", swap)
            terms = [(own, out_weight, 0, True), (other, other_weight, 0, False)]
            result = project(side_ref, terms, tokens, None, result, block_at, blocks)
            continue
        own = query_heads(
            block_at, queries, packed, near_now, local, rows, MID, pltpu.VMEM
        )
        other = lax.ppermute(own, "head", swap)
        terms = [(own, out_weight, 0, True), (other, other_weight, 0, False)]
        result = project(side_ref, terms, tokens, None, result, block_at, blocks, LEAN)
    return result


def solution(mesh):
    in_specs = (
        P(None, "tok", "head"),
        P(None, "tok", "head"),
        P(None, "tok", "head"),
        P("head", None, "tok"),
        P("head", None, None),
        P("head", None, None),
        P("head", None, None),
        P("head", None),
    )
    out_specs = P(None, "tok", "head")
    return jax.shard_map(shards, mesh=mesh, in_specs=in_specs, out_specs=out_specs, check_vma=False)
```
